32 devices in a mesh: dp: 4 (over z), fsdp: 8 (over y, x, core).
Axes of the slice: x: 2, y: 2, z: 4, core: 2. Of those that a mesh axis runs over, the one named last changes fastest.
Arguments:
- x_given: bfloat16 [65536, 768], P(('dp', 'fsdp')), may hold values from -6 to 6
- cotangent: bfloat16 [65536, 768], P(('dp', 'fsdp')), may hold values from -6 to 6
- norm_gain: bfloat16 [768], P(('dp', 'fsdp')), may hold values from 0.5 to 1.5
- w_qkv: bfloat16 [768, 2304], P(('dp', 'fsdp')), may hold values from -0.3125 to 0.3125
- w_out: bfloat16 [768, 768], P(('dp', 'fsdp')), may hold values from -1.5 to 1.5
- w_ada: bfloat16 [768, 2304], P(('dp', 'fsdp')), may hold values from -0.21875 to 0.21875
- w_up: bfloat16 [768, 3072], P(('dp', 'fsdp')), may hold values from -0.21875 to 0.21875
- w_down: bfloat16 [3072, 768], P(('dp', 'fsdp')), may hold values from -0.15625 to 0.15625
- seq_spans: int32 [128, 2], P(('dp', 'fsdp')), may hold values from 0 to 1024, as said below
- time_steps: int32 [128], P(('dp', 'fsdp')), may hold values from 0 to 999
- page_deal: int32 [4096], replicated, may hold values from 0 to 4095, as said below
Outputs:
- output: bfloat16 [65536, 768], P(('dp', 'fsdp'))
- input_grad: bfloat16 [65536, 768], P(('dp', 'fsdp'))
- gain_grad: float32 [768], P(('dp', 'fsdp'))
- qkv_grad: float32 [768, 2304], P(('dp', 'fsdp'))
- out_grad: float32 [768, 768], P(('dp', 'fsdp'))
- ada_grad: float32 [768, 2304], P(('dp', 'fsdp'))
- up_grad: float32 [768, 3072], P(('dp', 'fsdp'))
- down_grad: float32 [3072, 768], P(('dp', 'fsdp'))
The draws below stay inside these ranges and needn't reach their ends.
Inputs may be any that keep to these rules, and one draw needn't show every extreme that they name: seq_spans[j] = (start, length) of slot j, rows start to start + length - 1 of bin j // 2; slots of one bin don't intersect and end by 1024; a length may be 0; some bin holds one sequence of 1024 tokens. page_deal is a permutation; of the pages that one device holds in given order, the same number goes to every device.
All inputs are finite; a program needn't handle non-finite values.
Results may differ from the reference program's by a relative error of at most 0.014.
Values may be sent and summed in bfloat16 or wider, within the bound.
A program may use at most 320 MiB of HBM per device.

```python
import math
import jax
import jax.numpy as jnp
from jax import lax

D = 768
HEADS = 12
HEAD = 64
FF = 3072
BIN = 1024
SLOTS = 2
PAGE = 16
TSTEPS = 1000
SHARDS = 32
ROWS = 65536
PAGES = 4096
SEQS = 128


def draw_seq_spans(key, part):
    bin_count = ROWS // BIN
    subkeys = jax.random.split(jax.random.fold_in(key, 11), 5)
    used_rows = jax.random.randint(subkeys[0], (bin_count,), BIN // 2, BIN + 1)
    first_len = jax.random.randint(subkeys[1], (bin_count,), 0, used_rows + 1)
    leading = jax.random.randint(subkeys[2], (bin_count,), 0, BIN - used_rows + 1)
    middle = jax.random.randint(subkeys[3], (bin_count,), 0, BIN - used_rows - leading + 1)
    full_bin = jax.random.randint(subkeys[4], (), 0, bin_count)
    is_full = jnp.arange(bin_count) == full_bin
    used_rows = jnp.where(is_full, BIN, used_rows)
    first_len = jnp.where(is_full, BIN, first_len)
    leading = jnp.where(is_full, 0, leading)
    middle = jnp.where(is_full, 0, middle)
    starts = jnp.stack([leading, leading + first_len + middle], axis=1).reshape(-1)
    lengths = jnp.stack([first_len, used_rows - first_len], axis=1).reshape(-1)
    return jnp.stack([starts, lengths], axis=1).astype(jnp.int32)


def draw_page_deal(key, part):
    per_device = PAGES // SHARDS
    per_peer = per_device // SHARDS
    subkeys = jax.random.split(jax.random.fold_in(key, 23), 2)

    def shuffle(sub_key):
        return jax.random.permutation(sub_key, per_device)
    send_perm = jax.vmap(shuffle)(jax.random.split(subkeys[0], SHARDS))
    land_perm = jax.vmap(shuffle)(jax.random.split(subkeys[1], SHARDS))
    target = send_perm // per_peer
    incoming = jnp.arange(SHARDS)[:, None] * per_peer + send_perm % per_peer
    landing = land_perm[target, incoming]
    return (target * per_device + landing).reshape(-1).astype(jnp.int32)


def with_ends(drawn, key, least, largest):
    place = [jax.random.randint(jax.random.fold_in(key, axis), (), 0, length) for axis, length in enumerate(drawn.shape)]
    main_axis = drawn.shape.index(max(drawn.shape))
    neighbour = place[:main_axis] + [(place[main_axis] + 1) % drawn.shape[main_axis]] + place[main_axis + 1:]
    return drawn.at[tuple(place)].set(least).at[tuple(neighbour)].set(largest)


def levels(rng, extent, cuts, smallest, largest):
    def one(dim, parts):
        draws = jax.random.uniform(jax.random.fold_in(jax.random.fold_in(rng, 6), dim), (parts,), jnp.float32, smallest / len(cuts), largest / len(cuts))
        return jnp.repeat(jnp.exp(draws), extent[dim] // parts).reshape((-1,) + (1,) * (len(extent) - dim - 1))

    gain = one(*cuts[0])
    for cut in cuts[1:]:
        gain = gain * one(*cut)
    return gain


def gaussian(own_key, extent, deviation, limit, pieces=(), kind=jnp.bfloat16):
    level = levels(own_key, extent, pieces, -0.22, 0.18) if pieces else 1.0
    values = jax.random.normal(own_key, extent, jnp.float32) * deviation * level
    return jnp.minimum(jnp.maximum(values, -limit), limit).astype(kind)


def setup_inputs(seed: int = 0) -> dict:
    keys = jax.random.split(jax.random.key(seed), 12)
    return {
        "x_given": gaussian(keys[0], (ROWS, D), 1.0, 6.0, ((0, 32),)),
        "cotangent": gaussian(keys[1], (ROWS, D), 1.0, 6.0, ((0, 32),)),
        "norm_gain": jnp.clip(1.0 + 0.1 * jax.random.normal(keys[2], (D,), jnp.float32), 0.5, 1.5).astype(jnp.bfloat16),
        "w_qkv": gaussian(keys[3], (D, 3 * D), (D // 2) ** -0.5, 0.3125, ((0, 32),)),
        "w_out": gaussian(keys[4], (D, D), 16 ** -0.5, 1.5, ((0, 32),)),
        "w_ada": gaussian(keys[5], (D, 3 * D), D ** -0.5, 0.21875, ((0, 32),)),
        "w_up": gaussian(keys[6], (D, FF), D ** -0.5, 0.21875, ((0, 32),)),
        "w_down": gaussian(keys[7], (FF, D), (FF // 2) ** -0.5, 0.15625, ((0, 32),)),
        "seq_spans": draw_seq_spans(jax.random.fold_in(keys[11], 71), 0),
        "time_steps": with_ends(jax.random.randint(keys[9], (SEQS,), 0, TSTEPS), jax.random.fold_in(keys[9], 1), 0, TSTEPS - 1).astype(jnp.int32),
        "page_deal": draw_page_deal(jax.random.fold_in(keys[11], 71), 0),
    }


eps = 1e-05
neg_big = -1e+30
highest = lax.Precision.HIGHEST

@jax.custom_vjp
def low(v):
    return lax.optimization_barrier(v.astype(jnp.bfloat16)).astype(jnp.float32)

@jax.custom_vjp
def low_back(v):
    return v

def low_keep(v):
    return (low(v), None)

def low_pass(kept, grad):
    return (grad,)

def back_keep(v):
    return (v, None)

def back_low(kept, grad):
    return (low(grad),)
low.defvjp(low_keep, low_pass)
low_back.defvjp(back_keep, back_low)

def layer_norm(values, gain_vec):
    center = lax.optimization_barrier(jnp.mean(values, axis=-1, keepdims=True))
    shifted = values - center
    spread = lax.optimization_barrier(jnp.mean(shifted * shifted, axis=-1, keepdims=True))
    return shifted * lax.rsqrt(spread + eps) * gain_vec

def modulate(values, scale_rows, shift_rows):
    center = lax.optimization_barrier(jnp.mean(values, axis=-1, keepdims=True))
    shifted = values - center
    spread = lax.optimization_barrier(jnp.mean(shifted * shifted, axis=-1, keepdims=True))
    return shifted * lax.rsqrt(spread + eps) * (1.0 + scale_rows) + shift_rows

def gelu_tanh(values):
    return jax.nn.gelu(values, approximate=True)

def rope_tables(position, head_size):
    half_size = head_size // 2
    frequency = jnp.exp(jnp.arange(half_size, dtype=jnp.float32) * (-math.log(10000.0) / half_size))
    angles = position[:, None] * frequency[None, :]
    return (jnp.cos(angles), jnp.sin(angles))

def rotate(values, cosine, sine_table):
    half_size = values.shape[-1] // 2
    first_half = values[..., :half_size]
    second = values[..., half_size:]
    cos_rows = cosine[:, None, :]
    sin_rows = sine_table[:, None, :]
    return jnp.concatenate([first_half * cos_rows - second * sin_rows, second * cos_rows + first_half * sin_rows], axis=-1)

def time_features(time_steps, width):
    half_size = width // 2
    frequency = jnp.exp(jnp.arange(half_size, dtype=jnp.float32) * (-math.log(10000.0) / half_size))
    angles = time_steps.astype(jnp.float32)[:, None] * frequency[None, :]
    return jnp.concatenate([jnp.cos(angles), jnp.sin(angles)], axis=-1)

def row_layout(seq_spans, row_count):
    row_index = jnp.arange(row_count, dtype=jnp.int32)
    starts = seq_spans[:, 0]
    lengths = seq_spans[:, 1]
    offset = row_index[:, None] - starts[None, :]
    member = (offset >= 0) & (offset < lengths[None, :])
    slot_onehot = member.astype(jnp.float32)
    live_rows = lax.optimization_barrier(jnp.sum(slot_onehot, axis=1))
    slot_ids = jnp.arange(seq_spans.shape[0], dtype=jnp.int32)
    segment = lax.optimization_barrier(jnp.sum(jnp.where(member, slot_ids[None, :], 0), axis=1)) - jnp.where(jnp.any(member, axis=1), 0, 1)
    position = lax.optimization_barrier(jnp.sum(jnp.where(member, offset, 0), axis=1)).astype(jnp.float32)
    allowed = (segment[:, None] == segment[None, :]) & (segment[:, None] >= 0) | (row_index[:, None] == row_index[None, :])
    return (slot_onehot, live_rows, position, allowed)

def head_attention(query_head, key_head, value_head, allowed):
    scores = low_back(jnp.dot(query_head, key_head.T, precision=highest) * 0.125)
    masked = jnp.where(allowed, scores, neg_big)
    log_total = jax.nn.logsumexp(masked, axis=-1, keepdims=True)
    probs = jnp.exp(masked - log_total)
    return jnp.dot(low(probs), value_head, precision=highest)

def bin_forward(params, x_bin, spans_bin, steps_bin):
    gain_vec, qkv_mat, proj_mat, ada_mat, up_mat, down_mat = params
    row_count, width = x_bin.shape
    slot_onehot, live_rows, position, allowed = row_layout(spans_bin, row_count)
    time_feat = low(time_features(steps_bin, width))
    ada_seq = jnp.dot(time_feat, ada_mat, precision=highest)
    ada_rows = lax.optimization_barrier(jnp.sum(slot_onehot[:, :, None] * ada_seq[None, :, :], axis=1))
    scale_rows = ada_rows[:, :width]
    shift_rows = ada_rows[:, width:2 * width]
    gate_rows = ada_rows[:, 2 * width:]
    normed = low(layer_norm(x_bin, gain_vec))
    mixed_qkv = low_back(jnp.dot(normed, qkv_mat, precision=highest))
    cosine, sine_table = rope_tables(position, HEAD)
    queries = low(rotate(mixed_qkv[:, :width].reshape(row_count, HEADS, HEAD), cosine, sine_table))
    keys_rot = low(rotate(mixed_qkv[:, width:2 * width].reshape(row_count, HEADS, HEAD), cosine, sine_table))
    values_in = low(mixed_qkv[:, 2 * width:].reshape(row_count, HEADS, HEAD))

    def one_head(block):
        return head_attention(block[0], block[1], block[2], allowed)
    head_out = lax.map(jax.checkpoint(one_head), (jnp.transpose(queries, (1, 0, 2)), jnp.transpose(keys_rot, (1, 0, 2)), jnp.transpose(values_in, (1, 0, 2))))
    attended = low(low_back(jnp.transpose(head_out, (1, 0, 2)).reshape(row_count, width)))
    residual = x_bin + low_back(jnp.dot(attended, proj_mat, precision=highest))
    hidden_in = low(modulate(residual, scale_rows, shift_rows))
    pre_act = low_back(jnp.dot(hidden_in, up_mat, precision=highest))
    activation = low(gelu_tanh(pre_act))
    branch = low_back(jnp.dot(activation, down_mat, precision=highest))
    return (residual + gate_rows * branch) * live_rows[:, None]

def reference(x_given, cotangent, norm_gain, w_qkv, w_out, w_ada, w_up, w_down, seq_spans, time_steps, page_deal):
    page_count = page_deal.shape[0]
    inverse = jnp.zeros((page_count,), jnp.int32).at[page_deal].set(jnp.arange(page_count, dtype=jnp.int32))

    def to_dealt(values):
        return values.astype(jnp.float32).reshape(page_count, PAGE, D)[inverse].reshape(-1, BIN, D)
    x_bins = to_dealt(x_given)
    dy_bins = to_dealt(cotangent)
    bin_count = x_bins.shape[0]
    span_bins = seq_spans.reshape(bin_count, SLOTS, 2)
    step_bins = time_steps.reshape(bin_count, SLOTS)
    params = tuple((weight.astype(jnp.float32) for weight in (norm_gain, w_qkv, w_out, w_ada, w_up, w_down)))
    checked = jax.checkpoint(bin_forward)

    def forward(weights, inputs):

        def per_bin(block):
            return checked(weights, block[0], block[1], block[2])
        return lax.map(per_bin, (inputs, span_bins, step_bins))
    result, pull = jax.vjp(forward, params, x_bins)
    weight_grads, input_bins = pull(dy_bins)

    def to_given(values):
        return values.reshape(page_count, PAGE, D)[page_deal].reshape(-1, D)
    output = to_given(result).astype(jnp.bfloat16)
    input_grad = to_given(input_bins).astype(jnp.bfloat16)
    return (output, input_grad, weight_grads[0], weight_grads[1], weight_grads[2], weight_grads[3], weight_grads[4], weight_grads[5])
```

```python
import functools
import math

import jax
import jax.numpy as jnp
from jax import lax
from jax.experimental import pallas as pl
from jax.experimental.pallas import tpu as pltpu
from jax.sharding import PartitionSpec as P

D = 768
HEADS = 12
HEAD = 64
FF = 3072
BIN = 1024
MB = 2
SLOTS = 2
PAGE = 16
LANES = 128
PAIRS = HEADS // 2
ROWS = MB * BIN
CHUNK = 768
PIECE = 256
BLOCK = 256
VMEM_LIMIT = 60 << 20

eps = 1e-05
neg_big = -1e30
AXES = ("dp", "fsdp")
f32 = jnp.float32
bf16 = jnp.bfloat16

NN = (((1,), (0,)), ((), ()))
NT = (((1,), (1,)), ((), ()))
TN = (((0,), (0,)), ((), ()))


def mm(a, b, dims):
    return lax.dot_general(a, b, dims, preferred_element_type=f32)


def params(*semantics):
    return pltpu.CompilerParams(dimension_semantics=semantics, vmem_limit_bytes=VMEM_LIMIT)


def fixed(shape):
    return pl.BlockSpec(shape, lambda *g: (0,) * len(shape), pipeline_mode=pl.Buffered(1))


def normalise(values):
    center = jnp.mean(values, axis=-1, keepdims=True)
    shifted = values - center
    spread = jnp.mean(shifted * shifted, axis=-1, keepdims=True)
    inv = lax.rsqrt(spread + eps)
    return shifted * inv, inv


def partner(tile):
    lane = lax.broadcasted_iota(jnp.int32, tile.shape, 1)
    ahead = pltpu.roll(tile, LANES - HEAD // 2, 1)
    behind = pltpu.roll(tile, HEAD // 2, 1)
    return jnp.where(lane % HEAD < HEAD // 2, ahead, behind)


def qkv_body(x_ref, gain_ref, w_ref, cos_ref, sin_ref, qkv_ref, a1_ref):
    xhat, _ = normalise(x_ref[...].astype(f32))
    a1 = (xhat * gain_ref[0:1, :]).astype(bf16)
    a1_ref[...] = a1
    cosine, sine = cos_ref[...], sin_ref[...]
    for part in range(3):
        u = mm(a1, w_ref[:, part * D : (part + 1) * D], NN)
        for t in range(D // LANES):
            tile = u[:, t * LANES : (t + 1) * LANES]
            if part < 2:
                tile = tile * cosine + partner(tile) * sine
            if part == 0:
                tile = tile * 0.125
            at = part * D + t * LANES
            qkv_ref[:, at : at + LANES] = tile.astype(bf16)


def qkv_call(x, gain, w, cosine, sine):
    rows = x.shape[0]
    blk = 256
    return pl.pallas_call(
        qkv_body,
        name="qkv",
        grid=(rows // blk,),
        in_specs=[
            pl.BlockSpec((blk, D), lambda i: (i, 0)),
            fixed((8, D)),
            fixed((D, 3 * D)),
            pl.BlockSpec((blk, LANES), lambda i: (i, 0)),
            pl.BlockSpec((blk, LANES), lambda i: (i, 0)),
        ],
        out_specs=[
            pl.BlockSpec((blk, 3 * D), lambda i: (i, 0)),
            pl.BlockSpec((blk, D), lambda i: (i, 0)),
        ],
        out_shape=[
            jax.ShapeDtypeStruct((rows, 3 * D), bf16),
            jax.ShapeDtypeStruct((rows, D), bf16),
        ],
        compiler_params=params("arbitrary"),
        cost_estimate=pl.CostEstimate(
            flops=2 * rows * D * 3 * D, bytes_accessed=rows * D * 10, transcendentals=0
        ),
    )(x, gain, w, cosine, sine)


def attend_body(q_ref, k_ref, v_ref, qa_ref, ka_ref, p_ref, o_ref, rl_ref):
    pair = pl.program_id(1)
    blk = 256

    @pl.when(pair == 0)
    def _():
        rl_ref[...] = jnp.zeros_like(rl_ref)

    keys = jnp.concatenate([k_ref[...], ka_ref[...]], axis=1)
    vals = jnp.concatenate([v_ref[...], jnp.ones((BIN, LANES), bf16)], axis=1)
    lane = lax.broadcasted_iota(jnp.int32, (blk, LANES), 1)
    for rb in range(BIN // blk):
        rows = pl.ds(rb * blk, blk)
        q = q_ref[rows, :]
        outs = []
        for h in range(2):
            mine = (lane >= HEAD) == (h == 1)
            qh = jnp.concatenate([jnp.where(mine, q, jnp.zeros_like(q)), qa_ref[rows, :]], axis=1)
            s = mm(qh, keys, NT)
            top = jnp.max(s, axis=1, keepdims=True)
            p = jnp.exp(s - top).astype(bf16)
            p_ref[0, h, rows, :] = p
            ol = mm(p, vals, NN)
            rl = 1.0 / ol[:, LANES:]
            outs.append(ol[:, :LANES] * rl)
            rl_ref[rows, :] = jnp.where(lane == 2 * pair + h, rl, rl_ref[rows, :])
        o_ref[rows, :] = jnp.where(lane < HEAD, outs[0], outs[1]).astype(bf16)


def attend_call(qkv, qa, ka):
    bins = qkv.shape[0] // BIN
    tile = (BIN, LANES)
    return pl.pallas_call(
        attend_body,
        name="attend",
        grid=(bins, PAIRS),
        in_specs=[
            pl.BlockSpec(tile, lambda b, p: (b, p)),
            pl.BlockSpec(tile, lambda b, p: (b, PAIRS + p)),
            pl.BlockSpec(tile, lambda b, p: (b, 2 * PAIRS + p)),
            pl.BlockSpec(tile, lambda b, p: (b, 0)),
            pl.BlockSpec(tile, lambda b, p: (b, 0)),
        ],
        out_specs=[
            pl.BlockSpec((1, 2, BIN, BIN), lambda b, p: (b, p, 0, 0)),
            pl.BlockSpec(tile, lambda b, p: (b, p)),
            pl.BlockSpec(tile, lambda b, p: (b, 0)),
        ],
        out_shape=[
            jax.ShapeDtypeStruct((bins, HEADS, BIN, BIN), bf16),
            jax.ShapeDtypeStruct((bins * BIN, D), bf16),
            jax.ShapeDtypeStruct((bins * BIN, LANES), f32),
        ],
        compiler_params=params("arbitrary", "arbitrary"),
        cost_estimate=pl.CostEstimate(
            flops=bins * HEADS * BIN * BIN * 1024,
            bytes_accessed=bins * HEADS * BIN * BIN * 2,
            transcendentals=bins * HEADS * BIN * BIN,
        ),
    )(qkv, qkv, qkv, qa, ka)


def attend_back_body(
    q_ref, k_ref, v_ref, do_ref, o_ref, rl_ref, p_ref, cos_ref, sin_ref, dq_ref, dk_ref, dv_ref,
    dq_acc, dkt_acc, dvt_acc,
):
    pair = pl.program_id(1)
    blk = 256
    lane = lax.broadcasted_iota(jnp.int32, (blk, LANES), 1)
    lane_full = lax.broadcasted_iota(jnp.int32, (BIN, LANES), 1)

    def head(h, carry):
        vals = jnp.concatenate([v_ref[...], jnp.where(lane_full < 3, 1.0, 0.0).astype(bf16)], axis=1)
        mine = (lane >= HEAD) == (h == 1)
        dkt = jnp.zeros((LANES, BIN), f32)
        dvt = jnp.zeros((LANES, BIN), f32)
        for rb in range(BIN // blk):
            rows = pl.ds(rb * blk, blk)
            rl = jnp.sum(jnp.where(lane == 2 * pair + h, rl_ref[rows, :], 0.0), axis=1, keepdims=True)
            do = jnp.where(mine, do_ref[rows, :].astype(f32) * rl, 0.0).astype(bf16)
            delta = jnp.sum(do.astype(f32) * o_ref[rows, :].astype(f32), axis=1, keepdims=True)
            high = delta.astype(bf16).astype(f32)
            rest = delta - high
            mid = rest.astype(bf16).astype(f32)
            extra = jnp.where(lane == 0, -high, jnp.where(lane == 1, -mid, jnp.where(lane == 2, mid - rest, 0.0)))
            dp = mm(jnp.concatenate([do, extra.astype(bf16)], axis=1), vals, NT)
            p = p_ref[0, h, rows, :]
            ds = (p.astype(f32) * dp).astype(bf16)
            dq_acc[h, rows, :] = mm(ds, k_ref[...], NN)
            dkt += mm(q_ref[rows, :], ds, TN)
            dvt += mm(do, p, TN)
        dkt_acc[h] = dkt
        dvt_acc[h] = dvt
        return carry

    lax.fori_loop(0, 2, head, 0)
    sub = lax.broadcasted_iota(jnp.int32, (LANES, BIN), 0)
    dk = jnp.where(sub < HEAD, dkt_acc[0], dkt_acc[1]).T
    dv = jnp.where(sub < HEAD, dvt_acc[0], dvt_acc[1]).T
    cosine, sine = cos_ref[...], sin_ref[...]
    dq = jnp.where(lane_full < HEAD, dq_acc[0], dq_acc[1]) * 0.125
    dq_ref[...] = (dq * cosine - partner(dq) * sine).astype(bf16)
    dk_ref[...] = (dk * cosine - partner(dk) * sine).astype(bf16)
    dv_ref[...] = dv.astype(bf16)


def attend_back_call(qkv, do, o, rl, p, cosine, sine):
    bins = qkv.shape[0] // BIN
    tile = (BIN, LANES)
    grad = jax.ShapeDtypeStruct((bins * BIN, D), bf16)
    by_pair = pl.BlockSpec(tile, lambda b, p: (b, p))
    by_bin = pl.BlockSpec(tile, lambda b, p: (b, 0))
    return pl.pallas_call(
        attend_back_body,
        name="attend_back",
        grid=(bins, PAIRS),
        in_specs=[
            by_pair,
            pl.BlockSpec(tile, lambda b, p: (b, PAIRS + p)),
            pl.BlockSpec(tile, lambda b, p: (b, 2 * PAIRS + p)),
            by_pair,
            by_pair,
            by_bin,
            pl.BlockSpec((1, 2, BIN, BIN), lambda b, p: (b, p, 0, 0)),
            by_bin,
            by_bin,
        ],
        out_specs=[by_pair, by_pair, by_pair],
        out_shape=[grad, grad, grad],
        scratch_shapes=[
            pltpu.VMEM((2, BIN, LANES), f32),
            pltpu.VMEM((2, LANES, BIN), f32),
            pltpu.VMEM((2, LANES, BIN), f32),
        ],
        compiler_params=params("arbitrary", "arbitrary"),
        cost_estimate=pl.CostEstimate(
            flops=bins * HEADS * BIN * BIN * 2048,
            bytes_accessed=bins * HEADS * BIN * BIN * 2,
            transcendentals=0,
        ),
    )(qkv, qkv, qkv, do, o, rl, p, cosine, sine)


def rows_body(
    spans_ref, x_ref, o_ref, dy_ref, ada_ref, wo_ref, wu_ref, wd_ref,
    y_ref, dx1_ref, do_ref, dada_ref, go_hbm, gu_hbm, gd_hbm,
    go_acc, gu_acc, gd_acc, hb_ref, dmlp_ref, mlp_ref, dh_ref, stage_ref, sem,
):
    step = pl.program_id(0)
    last = pl.num_programs(0) - 1
    here = step // (BIN // BLOCK)
    first_row = (step % (BIN // BLOCK)) * BLOCK

    @pl.when(step == 0)
    def _():
        go_acc[...] = jnp.zeros_like(go_acc)
        gu_acc[...] = jnp.zeros_like(gu_acc)
        gd_acc[...] = jnp.zeros_like(gd_acc)
        dada_ref[...] = jnp.zeros_like(dada_ref)

    row = lax.broadcasted_iota(jnp.int32, (BLOCK, 1), 0) + first_row
    owned = []
    for k in range(SLOTS):
        start = spans_ref[here * SLOTS + k, 0]
        length = spans_ref[here * SLOTS + k, 1]
        owned.append(jnp.where((row >= start) & (row < start + length), 1.0, 0.0).astype(f32))
    live = owned[0] + owned[1]

    def ada(part):
        cols = slice(part * D, (part + 1) * D)
        return sum(owned[k] * ada_ref[pl.ds(here * SLOTS + k, 1), cols] for k in range(SLOTS))

    def add_slots(part, values):
        cols = slice(part * D, (part + 1) * D)
        for k in range(SLOTS):
            at = pl.ds(here * SLOTS + k, 1)
            dada_ref[at, cols] += jnp.sum(owned[k] * values, axis=0, keepdims=True)

    o = o_ref[...]
    x1 = x_ref[...].astype(f32) + mm(o, wo_ref[...], NN)
    xhat, inv = normalise(x1)
    one_scale = 1.0 + ada(0)
    hb_ref[...] = (xhat * one_scale + ada(1)).astype(bf16)
    gate = ada(2)
    dy = live * dy_ref[...].astype(f32)
    dmlp_ref[...] = (dy * gate).astype(bf16)
    mlp_ref[...] = jnp.zeros_like(mlp_ref)
    dh_ref[...] = jnp.zeros_like(dh_ref)
    c0 = math.sqrt(2.0 / math.pi)

    def chunk(c, carry):
        cols = pl.ds(pl.multiple_of(c * CHUNK, CHUNK), CHUNK)
        u = mm(hb_ref[...], wu_ref[:, cols], NN)
        uu = u * u
        t = jnp.tanh(u * (c0 + (c0 * 0.044715) * uu))
        half = 0.5 + 0.5 * t
        gb = (u * half).astype(bf16)
        mlp_ref[...] += mm(gb, wd_ref[cols, :], NN)
        gd_acc[cols, :] += mm(gb, dmlp_ref[...], TN)
        slope = half + (u * (1.0 - t * t)) * (0.5 * c0 + (1.5 * c0 * 0.044715) * uu)
        du = (mm(dmlp_ref[...], wd_ref[cols, :], NT) * slope).astype(bf16)
        dh_ref[...] += mm(du, wu_ref[:, cols], NT)
        gu_acc[:, cols] += mm(hb_ref[...], du, TN)
        return carry

    lax.fori_loop(0, FF // CHUNK, chunk, 0)
    mlp, dh = mlp_ref[...], dh_ref[...]
    y_ref[...] = (live * (x1 + gate * mlp)).astype(bf16)
    add_slots(2, dy * mlp)
    add_slots(1, dh)
    add_slots(0, dh * xhat)
    e = dh * one_scale
    dx1 = dy + (e - jnp.mean(e, axis=1, keepdims=True) - xhat * jnp.mean(e * xhat, axis=1, keepdims=True)) * inv
    dx1_ref[...] = dx1
    dattn = dx1.astype(bf16)
    go_acc[...] += mm(o, dattn, TN)
    do_ref[...] = mm(dattn, wo_ref[...], NT).astype(bf16)

    @pl.when(step == last)
    def _():
        pieces = []
        for acc, out in ((go_acc, go_hbm), (gu_acc, gu_hbm), (gd_acc, gd_hbm)):
            for r in range(0, acc.shape[0], PIECE):
                for c in range(0, acc.shape[1], D):
                    at = (slice(r, r + PIECE), slice(c, c + D))
                    pieces.append((acc.at[at], out.at[at]))
        copies = [None, None]
        for i, (acc, out) in enumerate(pieces):
            slot = i % 2
            if copies[slot] is not None:
                copies[slot].wait()
            stage_ref[slot] = acc[...].astype(bf16)
            copies[slot] = pltpu.make_async_copy(stage_ref.at[slot], out, sem.at[slot])
            copies[slot].start()
        for copy in copies:
            copy.wait()


def rows_call(spans, x, o, dy, ada, w_out, w_up, w_down):
    rows = x.shape[0]
    block = pl.BlockSpec((BLOCK, D), lambda i, s: (i, 0))
    anywhere = pl.BlockSpec(memory_space=pl.ANY)
    return pl.pallas_call(
        rows_body,
        name="rows",
        grid_spec=pltpu.PrefetchScalarGridSpec(
            num_scalar_prefetch=1,
            grid=(rows // BLOCK,),
            in_specs=[
                block, block, block, fixed((8, 3 * D)), fixed((D, D)), fixed((D, FF)), fixed((FF, D)),
            ],
            out_specs=[
                block, block, block, pl.BlockSpec((8, 3 * D), lambda i, s: (0, 0)), anywhere, anywhere, anywhere,
            ],
            scratch_shapes=[
                pltpu.VMEM((D, D), f32),
                pltpu.VMEM((D, FF), f32),
                pltpu.VMEM((FF, D), f32),
                pltpu.VMEM((BLOCK, D), bf16),
                pltpu.VMEM((BLOCK, D), bf16),
                pltpu.VMEM((BLOCK, D), f32),
                pltpu.VMEM((BLOCK, D), f32),
                pltpu.VMEM((2, PIECE, D), bf16),
                pltpu.SemaphoreType.DMA((2,)),
            ],
        ),
        out_shape=[
            jax.ShapeDtypeStruct((rows, D), bf16),
            jax.ShapeDtypeStruct((rows, D), f32),
            jax.ShapeDtypeStruct((rows, D), bf16),
            jax.ShapeDtypeStruct((8, 3 * D), f32),
            jax.ShapeDtypeStruct((D, D), bf16),
            jax.ShapeDtypeStruct((D, FF), bf16),
            jax.ShapeDtypeStruct((FF, D), bf16),
        ],
        compiler_params=params("arbitrary"),
        cost_estimate=pl.CostEstimate(
            flops=6 * rows * D * (D + 2 * FF), bytes_accessed=rows * D * 14, transcendentals=rows * FF
        ),
    )(spans, x, o, dy, ada, w_out, w_up, w_down)


def qkv_back_body(x_ref, dx1_ref, dq_ref, dk_ref, dv_ref, gain_ref, w_ref, dx_ref, gg_ref):
    @pl.when(pl.program_id(0) == 0)
    def _():
        gg_ref[...] = jnp.zeros_like(gg_ref)

    xhat, inv = normalise(x_ref[...].astype(f32))
    dn = mm(dq_ref[...], w_ref[:, :D], NT)
    dn += mm(dk_ref[...], w_ref[:, D : 2 * D], NT)
    dn += mm(dv_ref[...], w_ref[:, 2 * D :], NT)
    gg_ref[0:1, :] += jnp.sum(dn * xhat, axis=0, keepdims=True)
    e = dn * gain_ref[0:1, :]
    back = (e - jnp.mean(e, axis=1, keepdims=True) - xhat * jnp.mean(e * xhat, axis=1, keepdims=True)) * inv
    dx_ref[...] = (dx1_ref[...] + back).astype(bf16)


def qkv_back_call(x, dx1, dq, dk, dv, gain, w):
    rows = x.shape[0]
    blk = 256
    block = pl.BlockSpec((blk, D), lambda i: (i, 0))
    return pl.pallas_call(
        qkv_back_body,
        name="qkv_back",
        grid=(rows // blk,),
        in_specs=[block, block, block, block, block, fixed((8, D)), fixed((D, 3 * D))],
        out_specs=[block, pl.BlockSpec((8, D), lambda i: (0, 0))],
        out_shape=[jax.ShapeDtypeStruct((rows, D), bf16), jax.ShapeDtypeStruct((8, D), f32)],
        compiler_params=params("arbitrary"),
        cost_estimate=pl.CostEstimate(
            flops=2 * rows * D * 3 * D, bytes_accessed=rows * D * 14, transcendentals=0
        ),
    )(x, dx1, dq, dk, dv, gain, w)


def qkv_grad_body(a1_ref, dq_ref, dk_ref, dv_ref, out_ref, acc_ref):
    step = pl.program_id(0)

    @pl.when(step == 0)
    def _():
        acc_ref[...] = jnp.zeros_like(acc_ref)

    a1 = a1_ref[...]
    for part, ref in enumerate((dq_ref, dk_ref, dv_ref)):
        acc_ref[:, part * D : (part + 1) * D] += mm(a1, ref[...], TN)

    @pl.when(step == pl.num_programs(0) - 1)
    def _():
        out_ref[...] = acc_ref[...].astype(bf16)


def qkv_grad_call(a1, dq, dk, dv):
    rows = a1.shape[0]
    blk = 512
    block = pl.BlockSpec((blk, D), lambda i: (i, 0))
    return pl.pallas_call(
        qkv_grad_body,
        name="qkv_grad",
        grid=(rows // blk,),
        in_specs=[block, block, block, block],
        out_specs=pl.BlockSpec((D, 3 * D), lambda i: (0, 0)),
        out_shape=jax.ShapeDtypeStruct((D, 3 * D), bf16),
        scratch_shapes=[pltpu.VMEM((D, 3 * D), f32)],
        compiler_params=params("arbitrary"),
        cost_estimate=pl.CostEstimate(
            flops=2 * rows * D * 3 * D, bytes_accessed=rows * D * 8, transcendentals=0
        ),
    )(a1, dq, dk, dv)


def feature_angles(time_steps, width):
    half = width // 2
    frequency = jnp.exp(jnp.arange(half, dtype=f32) * (-math.log(10000.0) / half))
    return time_steps.astype(f32)[:, None] * frequency[None, :]


def time_features(time_steps, width):
    angles = feature_angles(time_steps, width)
    return jnp.concatenate([jnp.cos(angles), jnp.sin(angles)], axis=-1).astype(bf16)


def row_tables(seq_spans):
    row = jnp.arange(BIN, dtype=jnp.int32)[None, :, None]
    spans = seq_spans.reshape(MB, 1, SLOTS, 2)
    offset = row - spans[..., 0]
    member = (offset >= 0) & (offset < spans[..., 1])
    position = jnp.sum(jnp.where(member, offset, 0), axis=2).astype(f32).reshape(ROWS, 1)
    lane = jnp.arange(LANES, dtype=jnp.int32)[None, :]
    half = HEAD // 2
    frequency = jnp.exp((lane % half).astype(f32) * (-math.log(10000.0) / half))
    angle = position * frequency
    cosine = jnp.cos(angle)
    sine = jnp.sin(angle) * jnp.where(lane % HEAD < half, -1.0, 1.0)
    member = member.reshape(ROWS, SLOTS)
    slot = jnp.arange(LANES, dtype=jnp.int32)[None, :]
    mine = jnp.sum(jnp.where((slot[:, None, :] == jnp.arange(SLOTS)[None, :, None]), member[:, :, None], False), axis=1)
    query_mask = jnp.where(mine > 0, neg_big, 0.0).astype(bf16)
    key_mask = jnp.where((mine == 0) & (slot < SLOTS), 1.0, 0.0).astype(bf16)
    return cosine, sine, query_mask, key_mask


def page_plan(page_deal, pages_dev, shards, device):
    per_peer = pages_dev // shards
    ids = jnp.arange(pages_dev, dtype=jnp.int32)
    deal = lax.dynamic_slice_in_dim(page_deal, device * pages_dev, pages_dev)
    target = deal // pages_dev
    earlier = (target[:, None] == target[None, :]) & (deal[None, :] < deal[:, None])
    send_pos = target * per_peer + jnp.sum(earlier.astype(jnp.int32), axis=1)
    send_order = jnp.sum(jnp.where(send_pos[None, :] == ids[:, None], ids[None, :], 0), axis=1)
    all_ids = jnp.arange(page_deal.shape[0], dtype=jnp.int32)
    hit = page_deal[None, :] == (device * pages_dev + ids)[:, None]
    owned = jnp.sum(jnp.where(hit, all_ids[None, :], 0), axis=1)
    source = owned // pages_dev
    before = (source[:, None] == source[None, :]) & (ids[None, :] < ids[:, None])
    recv_pos = source * per_peer + jnp.sum(before.astype(jnp.int32), axis=1)
    recv_order = jnp.sum(jnp.where(recv_pos[None, :] == ids[:, None], ids[None, :], 0), axis=1)
    return send_pos, send_order, recv_pos, recv_order


def pages(values):
    return values.reshape(-1, PAGE, D)


def exchange(values, shards):
    sent = values.reshape(shards, -1, PAGE, D)
    got = lax.all_to_all(sent, AXES, split_axis=0, concat_axis=0, tiled=True)
    return got.reshape(-1, PAGE, D)


def per_device(
    x_given, cotangent, norm_gain, w_qkv, w_out, w_ada, w_up, w_down, seq_spans, time_steps, page_deal
):
    shards = lax.axis_size(AXES)
    device = lax.axis_index(AXES)
    rows_dev = x_given.shape[0]
    pages_dev = rows_dev // PAGE
    send_pos, send_order, recv_pos, recv_order = page_plan(page_deal, pages_dev, shards, device)
    x = exchange(pages(x_given)[send_order], shards)[recv_pos].reshape(rows_dev, D)
    dy = exchange(pages(cotangent)[send_order], shards)[recv_pos].reshape(rows_dev, D)

    def gather(w):
        return lax.all_gather(w, AXES, axis=0, tiled=True)

    qkv_all = gather(w_qkv)
    ada_ext = jnp.concatenate([w_ada, jnp.broadcast_to(norm_gain[:, None], (norm_gain.shape[0], LANES))], axis=1)
    ada_ext = gather(ada_ext)
    out_all, up_all, down_all = gather(w_out), gather(w_up), gather(w_down)
    ada_all = ada_ext[:, : 3 * D]
    gain = jnp.broadcast_to(ada_ext[:, 3 * D].astype(f32)[None, :], (8, D))

    cosine, sine, query_mask, key_mask = row_tables(seq_spans)
    time_feat = time_features(time_steps, D)
    ada_seq = jnp.dot(time_feat, ada_all, preferred_element_type=f32)
    ada_seq = jnp.concatenate([ada_seq, jnp.zeros_like(ada_seq)], axis=0)

    qkv, a1 = qkv_call(x, gain, qkv_all, cosine, sine)
    p, o, rl = attend_call(qkv, query_mask, key_mask)
    y, dx1, do, dada, go, gu, gd = rows_call(seq_spans, x, o, dy, ada_seq, out_all, up_all, down_all)

    output = exchange(pages(y)[recv_order], shards)[send_pos].reshape(rows_dev, D)

    def reduce(g):
        return lax.psum_scatter(g, AXES, scatter_dimension=0, tiled=True)

    up_grad, down_grad, out_grad = reduce(gu), reduce(gd), reduce(go)
    slots = time_steps.shape[0]
    steps_col = jnp.broadcast_to(time_steps.astype(f32)[:, None], (slots, LANES))
    slot_rows = jnp.concatenate([dada[:slots], steps_col], axis=1)
    slot_all = lax.all_gather(slot_rows, AXES, axis=0, tiled=True)
    own = norm_gain.shape[0]
    half = D // 2
    feature = device * own + jnp.arange(own, dtype=jnp.int32)
    frequency = jnp.exp((feature % half).astype(f32) * (-math.log(10000.0) / half))
    angle = slot_all[:, 3 * D : 3 * D + 1] * frequency[None, :]
    feat_own = jnp.where(feature[None, :] < half, jnp.cos(angle), jnp.sin(angle)).astype(bf16).astype(f32)
    ada_grad = lax.dot_general(feat_own, slot_all[:, : 3 * D], TN, precision=lax.Precision.HIGHEST)

    dq, dk, dv = attend_back_call(qkv, do, o, rl, p, cosine, sine)
    dx, gg = qkv_back_call(x, dx1, dq, dk, dv, gain, qkv_all)
    input_grad = exchange(pages(dx)[recv_order], shards)[send_pos].reshape(rows_dev, D)
    gq = qkv_grad_call(a1, dq, dk, dv)
    gq = jnp.concatenate([gq, jnp.broadcast_to(gg[0].astype(bf16)[:, None], (D, LANES))], axis=1)
    gq = reduce(gq)
    return (
        output,
        input_grad,
        gq[:, 3 * D].astype(f32),
        gq[:, : 3 * D].astype(f32),
        out_grad.astype(f32),
        ada_grad,
        up_grad.astype(f32),
        down_grad.astype(f32),
    )


def solution(mesh):
    placed = P(AXES, None)
    vector = P(AXES)
    return jax.shard_map(
        per_device,
        mesh=mesh,
        in_specs=(placed, placed, vector, placed, placed, placed, placed, placed, placed, vector, P()),
        out_specs=(placed, placed, vector, placed, placed, placed, placed, placed),
        check_vma=False,
    )
```

```python
import functools
import math

import jax
import jax.numpy as jnp
from jax import lax
from jax.experimental import pallas as pl
from jax.experimental.pallas import tpu as pltpu
from jax.sharding import PartitionSpec as P

D = 768
HEADS = 12
HEAD = 64
FF = 3072
BIN = 1024
MB = 2
SLOTS = 2
PAGE = 16
LANES = 128
GAIN_COLS = 128
PAIRS = HEADS // 2
ROWS = MB * BIN
CHUNK = 768
PIECE = 256
BLOCK = 256
VMEM_LIMIT = 60 << 20

eps = 1e-05
neg_big = -1e30
AXES = ("dp", "fsdp")
f32 = jnp.float32
bf16 = jnp.bfloat16

NN = (((1,), (0,)), ((), ()))
NT = (((1,), (1,)), ((), ()))
TN = (((0,), (0,)), ((), ()))


def mm(a, b, dims):
    return lax.dot_general(a, b, dims, preferred_element_type=f32)


def params(*semantics):
    return pltpu.CompilerParams(dimension_semantics=semantics, vmem_limit_bytes=VMEM_LIMIT)


def fixed(shape):
    return pl.BlockSpec(shape, lambda *g: (0,) * len(shape), pipeline_mode=pl.Buffered(1))


def normalise(values):
    center = jnp.mean(values, axis=-1, keepdims=True)
    shifted = values - center
    spread = jnp.mean(shifted * shifted, axis=-1, keepdims=True)
    inv = lax.rsqrt(spread + eps)
    return shifted * inv, inv


def partner(tile):
    lane = lax.broadcasted_iota(jnp.int32, tile.shape, 1)
    ahead = pltpu.roll(tile, LANES - HEAD // 2, 1)
    behind = pltpu.roll(tile, HEAD // 2, 1)
    return jnp.where(lane % HEAD < HEAD // 2, ahead, behind)


def qkv_body(x_ref, gain_ref, w_ref, cos_ref, sin_ref, qkv_ref, a1_ref):
    xhat, _ = normalise(x_ref[...].astype(f32))
    a1 = (xhat * gain_ref[0:1, :]).astype(bf16)
    a1_ref[...] = a1
    cosine, sine = cos_ref[...], sin_ref[...]
    for part in range(3):
        u = mm(a1, w_ref[:, part * D : (part + 1) * D], NN)
        for t in range(D // LANES):
            tile = u[:, t * LANES : (t + 1) * LANES]
            if part < 2:
                tile = tile * cosine + partner(tile) * sine
            if part == 0:
                tile = tile * 0.125
            at = part * D + t * LANES
            qkv_ref[:, at : at + LANES] = tile.astype(bf16)


def qkv_call(x, gain, w, cosine, sine):
    rows = x.shape[0]
    blk = 256
    return pl.pallas_call(
        qkv_body,
        name="qkv",
        grid=(rows // blk,),
        in_specs=[
            pl.BlockSpec((blk, D), lambda i: (i, 0)),
            fixed((8, D)),
            fixed((D, 3 * D)),
            pl.BlockSpec((blk, LANES), lambda i: (i, 0)),
            pl.BlockSpec((blk, LANES), lambda i: (i, 0)),
        ],
        out_specs=[
            pl.BlockSpec((blk, 3 * D), lambda i: (i, 0)),
            pl.BlockSpec((blk, D), lambda i: (i, 0)),
        ],
        out_shape=[
            jax.ShapeDtypeStruct((rows, 3 * D), bf16),
            jax.ShapeDtypeStruct((rows, D), bf16),
        ],
        compiler_params=params("arbitrary"),
        cost_estimate=pl.CostEstimate(
            flops=2 * rows * D * 3 * D, bytes_accessed=rows * D * 10, transcendentals=0
        ),
    )(x, gain, w, cosine, sine)


def attend_body(q_ref, k_ref, v_ref, qa_ref, ka_ref, p_ref, o_ref, rl_ref):
    pair = pl.program_id(1)
    blk = 256

    @pl.when(pair == 0)
    def _():
        rl_ref[...] = jnp.zeros_like(rl_ref)

    keys = jnp.concatenate([k_ref[...], ka_ref[...]], axis=1)
    vals = jnp.concatenate([v_ref[...], jnp.ones((BIN, LANES), bf16)], axis=1)
    lane = lax.broadcasted_iota(jnp.int32, (blk, LANES), 1)
    for rb in range(BIN // blk):
        rows = pl.ds(rb * blk, blk)
        q = q_ref[rows, :]
        outs = []
        for h in range(2):
            mine = (lane >= HEAD) == (h == 1)
            qh = jnp.concatenate([jnp.where(mine, q, jnp.zeros_like(q)), qa_ref[rows, :]], axis=1)
            s = mm(qh, keys, NT)
            top = jnp.max(s, axis=1, keepdims=True)
            p = jnp.exp(s - top).astype(bf16)
            p_ref[0, h, rows, :] = p
            ol = mm(p, vals, NN)
            rl = 1.0 / ol[:, LANES:]
            outs.append(ol[:, :LANES] * rl)
            rl_ref[rows, :] = jnp.where(lane == 2 * pair + h, rl, rl_ref[rows, :])
        o_ref[rows, :] = jnp.where(lane < HEAD, outs[0], outs[1]).astype(bf16)


def attend_call(qkv, qa, ka):
    bins = qkv.shape[0] // BIN
    tile = (BIN, LANES)
    return pl.pallas_call(
        attend_body,
        name="attend",
        grid=(bins, PAIRS),
        in_specs=[
            pl.BlockSpec(tile, lambda b, p: (b, p)),
            pl.BlockSpec(tile, lambda b, p: (b, PAIRS + p)),
            pl.BlockSpec(tile, lambda b, p: (b, 2 * PAIRS + p)),
            pl.BlockSpec(tile, lambda b, p: (b, 0)),
            pl.BlockSpec(tile, lambda b, p: (b, 0)),
        ],
        out_specs=[
            pl.BlockSpec((1, 2, BIN, BIN), lambda b, p: (b, p, 0, 0)),
            pl.BlockSpec(tile, lambda b, p: (b, p)),
            pl.BlockSpec(tile, lambda b, p: (b, 0)),
        ],
        out_shape=[
            jax.ShapeDtypeStruct((bins, HEADS, BIN, BIN), bf16),
            jax.ShapeDtypeStruct((bins * BIN, D), bf16),
            jax.ShapeDtypeStruct((bins * BIN, LANES), f32),
        ],
        compiler_params=params("arbitrary", "arbitrary"),
        cost_estimate=pl.CostEstimate(
            flops=bins * HEADS * BIN * BIN * 1024,
            bytes_accessed=bins * HEADS * BIN * BIN * 2,
            transcendentals=bins * HEADS * BIN * BIN,
        ),
    )(qkv, qkv, qkv, qa, ka)


def attend_back_body(
    q_ref, k_ref, v_ref, do_ref, o_ref, rl_ref, p_ref, cos_ref, sin_ref, dq_ref, dk_ref, dv_ref,
    dq_acc, dkt_acc, dvt_acc,
):
    pair = pl.program_id(1)
    blk = 256
    lane = lax.broadcasted_iota(jnp.int32, (blk, LANES), 1)
    lane_full = lax.broadcasted_iota(jnp.int32, (BIN, LANES), 1)

    def head(h, carry):
        vals = jnp.concatenate([v_ref[...], jnp.where(lane_full < 3, 1.0, 0.0).astype(bf16)], axis=1)
        mine = (lane >= HEAD) == (h == 1)
        dkt = jnp.zeros((LANES, BIN), f32)
        dvt = jnp.zeros((LANES, BIN), f32)
        for rb in range(BIN // blk):
            rows = pl.ds(rb * blk, blk)
            rl = jnp.sum(jnp.where(lane == 2 * pair + h, rl_ref[rows, :], 0.0), axis=1, keepdims=True)
            do = jnp.where(mine, do_ref[rows, :].astype(f32) * rl, 0.0).astype(bf16)
            delta = jnp.sum(do.astype(f32) * o_ref[rows, :].astype(f32), axis=1, keepdims=True)
            high = delta.astype(bf16).astype(f32)
            rest = delta - high
            mid = rest.astype(bf16).astype(f32)
            extra = jnp.where(lane == 0, -high, jnp.where(lane == 1, -mid, jnp.where(lane == 2, mid - rest, 0.0)))
            dp = mm(jnp.concatenate([do, extra.astype(bf16)], axis=1), vals, NT)
            p = p_ref[0, h, rows, :]
            ds = (p.astype(f32) * dp).astype(bf16)
            dq_acc[h, rows, :] = mm(ds, k_ref[...], NN)
            dkt += mm(q_ref[rows, :], ds, TN)
            dvt += mm(do, p, TN)
        dkt_acc[h] = dkt
        dvt_acc[h] = dvt
        return carry

    lax.fori_loop(0, 2, head, 0)
    sub = lax.broadcasted_iota(jnp.int32, (LANES, BIN), 0)
    dk = jnp.where(sub < HEAD, dkt_acc[0], dkt_acc[1]).T
    dv = jnp.where(sub < HEAD, dvt_acc[0], dvt_acc[1]).T
    cosine, sine = cos_ref[...], sin_ref[...]
    dq = jnp.where(lane_full < HEAD, dq_acc[0], dq_acc[1]) * 0.125
    dq_ref[...] = (dq * cosine - partner(dq) * sine).astype(bf16)
    dk_ref[...] = (dk * cosine - partner(dk) * sine).astype(bf16)
    dv_ref[...] = dv.astype(bf16)


def attend_back_call(qkv, do, o, rl, p, cosine, sine):
    bins = qkv.shape[0] // BIN
    tile = (BIN, LANES)
    grad = jax.ShapeDtypeStruct((bins * BIN, D), bf16)
    by_pair = pl.BlockSpec(tile, lambda b, p: (b, p))
    by_bin = pl.BlockSpec(tile, lambda b, p: (b, 0))
    return pl.pallas_call(
        attend_back_body,
        name="attend_back",
        grid=(bins, PAIRS),
        in_specs=[
            by_pair,
            pl.BlockSpec(tile, lambda b, p: (b, PAIRS + p)),
            pl.BlockSpec(tile, lambda b, p: (b, 2 * PAIRS + p)),
            by_pair,
            by_pair,
            by_bin,
            pl.BlockSpec((1, 2, BIN, BIN), lambda b, p: (b, p, 0, 0)),
            by_bin,
            by_bin,
        ],
        out_specs=[by_pair, by_pair, by_pair],
        out_shape=[grad, grad, grad],
        scratch_shapes=[
            pltpu.VMEM((2, BIN, LANES), f32),
            pltpu.VMEM((2, LANES, BIN), f32),
            pltpu.VMEM((2, LANES, BIN), f32),
        ],
        compiler_params=params("arbitrary", "arbitrary"),
        cost_estimate=pl.CostEstimate(
            flops=bins * HEADS * BIN * BIN * 2048,
            bytes_accessed=bins * HEADS * BIN * BIN * 2,
            transcendentals=0,
        ),
    )(qkv, qkv, qkv, do, o, rl, p, cosine, sine)


def rows_body(
    spans_ref, x_ref, o_ref, dy_ref, ada_ref, feat_ref, wo_ref, wu_ref, wd_ref,
    y_ref, dx1_ref, do_ref, grads_hbm,
    go_acc, gu_acc, gd_acc, dada_ref, hb_ref, dmlp_ref, mlp_ref, dh_ref, stage_ref, sem,
):
    step = pl.program_id(0)
    last = pl.num_programs(0) - 1
    here = step // (BIN // BLOCK)
    first_row = (step % (BIN // BLOCK)) * BLOCK

    @pl.when(step == 0)
    def _():
        go_acc[...] = jnp.zeros_like(go_acc)
        gu_acc[...] = jnp.zeros_like(gu_acc)
        gd_acc[...] = jnp.zeros_like(gd_acc)
        dada_ref[...] = jnp.zeros_like(dada_ref)

    row = lax.broadcasted_iota(jnp.int32, (BLOCK, 1), 0) + first_row
    owned = []
    for k in range(SLOTS):
        start = spans_ref[here * SLOTS + k, 0]
        length = spans_ref[here * SLOTS + k, 1]
        owned.append(jnp.where((row >= start) & (row < start + length), 1.0, 0.0).astype(f32))
    live = owned[0] + owned[1]

    def ada(part):
        cols = slice(part * D, (part + 1) * D)
        return sum(owned[k] * ada_ref[pl.ds(here * SLOTS + k, 1), cols] for k in range(SLOTS))

    def add_slots(part, values):
        cols = slice(part * D, (part + 1) * D)
        for k in range(SLOTS):
            at = pl.ds(here * SLOTS + k, 1)
            dada_ref[at, cols] += jnp.sum(owned[k] * values, axis=0, keepdims=True)

    o = o_ref[...]
    x1 = x_ref[...].astype(f32) + mm(o, wo_ref[...], NN)
    xhat, inv = normalise(x1)
    one_scale = 1.0 + ada(0)
    hb_ref[...] = (xhat * one_scale + ada(1)).astype(bf16)
    gate = ada(2)
    dy = live * dy_ref[...].astype(f32)
    dmlp_ref[...] = (dy * gate).astype(bf16)
    mlp_ref[...] = jnp.zeros_like(mlp_ref)
    dh_ref[...] = jnp.zeros_like(dh_ref)
    c0 = math.sqrt(2.0 / math.pi)

    def chunk(c, carry):
        cols = pl.ds(pl.multiple_of(c * CHUNK, CHUNK), CHUNK)
        u = mm(hb_ref[...], wu_ref[:, cols], NN)
        uu = u * u
        t = jnp.tanh(u * (c0 + (c0 * 0.044715) * uu))
        half = 0.5 + 0.5 * t
        gb = (u * half).astype(bf16)
        mlp_ref[...] += mm(gb, wd_ref[:, cols], NN)
        gd_acc[:, cols] += mm(gb, dmlp_ref[...], TN)
        slope = half + (u * (1.0 - t * t)) * (0.5 * c0 + (1.5 * c0 * 0.044715) * uu)
        du = (mm(dmlp_ref[...], wd_ref[:, cols], NT) * slope).astype(bf16)
        dh_ref[...] += mm(du, wu_ref[:, cols], NT)
        gu_acc[:, cols] += mm(hb_ref[...], du, TN)
        return carry

    lax.fori_loop(0, FF // CHUNK, chunk, 0)
    mlp, dh = mlp_ref[...], dh_ref[...]
    y_ref[...] = (live * (x1 + gate * mlp)).astype(bf16)
    add_slots(2, dy * mlp)
    add_slots(1, dh)
    add_slots(0, dh * xhat)
    e = dh * one_scale
    dx1 = dy + (e - jnp.mean(e, axis=1, keepdims=True) - xhat * jnp.mean(e * xhat, axis=1, keepdims=True)) * inv
    dx1_ref[...] = dx1
    dattn = dx1.astype(bf16)
    go_acc[...] += mm(o, dattn, TN)
    do_ref[...] = mm(dattn, wo_ref[...], NT).astype(bf16)

    @pl.when(step == last)
    def _():
        high = dada_ref[...].astype(bf16)
        low = (dada_ref[...] - high.astype(f32)).astype(bf16)
        sums = jnp.concatenate([high, low], axis=0)

        def slots_grad(r, c):
            return mm(feat_ref[:, r : r + PIECE], sums[:, c : c + D], TN)

        def held(acc):
            return lambda r, c: acc[r : r + PIECE, c : c + D]

        pieces = []
        for piece, first, width in (
            (held(gu_acc), 0, FF),
            (held(gd_acc), FF, FF),
            (held(go_acc), 2 * FF, D),
            (slots_grad, 2 * FF + D, 3 * D),
        ):
            for r in range(0, D, PIECE):
                for c in range(0, width, D):
                    pieces.append((piece, r, c, grads_hbm.at[r : r + PIECE, first + c : first + c + D]))
        copies = [None, None]
        for i, (piece, r, c, out) in enumerate(pieces):
            slot = i % 2
            if copies[slot] is not None:
                copies[slot].wait()
            stage_ref[slot] = piece(r, c).astype(bf16)
            copies[slot] = pltpu.make_async_copy(stage_ref.at[slot], out, sem.at[slot])
            copies[slot].start()
        for copy in copies:
            copy.wait()


def columns(width, index):
    return pl.BlockSpec((D, width), lambda *g: (0, index), pipeline_mode=pl.Buffered(1))


def rows_call(spans, x, o, dy, ada, feat, weights):
    rows = x.shape[0]
    block = pl.BlockSpec((BLOCK, D), lambda i, s: (i, 0))
    anywhere = pl.BlockSpec(memory_space=pl.ANY)
    return pl.pallas_call(
        rows_body,
        name="rows",
        grid_spec=pltpu.PrefetchScalarGridSpec(
            num_scalar_prefetch=1,
            grid=(rows // BLOCK,),
            in_specs=[
                block, block, block, fixed((8, 3 * D)), fixed((16, D)),
                columns(D, 2 * FF // D), columns(FF, 0), columns(FF, 1),
            ],
            out_specs=[
                block, block, block, anywhere,
            ],
            scratch_shapes=[
                pltpu.VMEM((D, D), f32),
                pltpu.VMEM((D, FF), f32),
                pltpu.VMEM((D, FF), f32),
                pltpu.VMEM((8, 3 * D), f32),
                pltpu.VMEM((BLOCK, D), bf16),
                pltpu.VMEM((BLOCK, D), bf16),
                pltpu.VMEM((BLOCK, D), f32),
                pltpu.VMEM((BLOCK, D), f32),
                pltpu.VMEM((2, PIECE, D), bf16),
                pltpu.SemaphoreType.DMA((2,)),
            ],
        ),
        out_shape=[
            jax.ShapeDtypeStruct((rows, D), bf16),
            jax.ShapeDtypeStruct((rows, D), f32),
            jax.ShapeDtypeStruct((rows, D), bf16),
            jax.ShapeDtypeStruct((D, 2 * FF + 4 * D), bf16),
        ],
        compiler_params=params("arbitrary"),
        cost_estimate=pl.CostEstimate(
            flops=6 * rows * D * (D + 2 * FF), bytes_accessed=rows * D * 14, transcendentals=rows * FF
        ),
    )(spans, x, o, dy, ada, feat, weights, weights, weights)


def qkv_back_body(x_ref, dx1_ref, dq_ref, dk_ref, dv_ref, gain_ref, w_ref, dx_ref, gg_ref):
    @pl.when(pl.program_id(0) == 0)
    def _():
        gg_ref[...] = jnp.zeros_like(gg_ref)

    xhat, inv = normalise(x_ref[...].astype(f32))
    dn = mm(dq_ref[...], w_ref[:, :D], NT)
    dn += mm(dk_ref[...], w_ref[:, D : 2 * D], NT)
    dn += mm(dv_ref[...], w_ref[:, 2 * D :], NT)
    gg_ref[0:1, :] += jnp.sum(dn * xhat, axis=0, keepdims=True)
    e = dn * gain_ref[0:1, :]
    back = (e - jnp.mean(e, axis=1, keepdims=True) - xhat * jnp.mean(e * xhat, axis=1, keepdims=True)) * inv
    dx_ref[...] = (dx1_ref[...] + back).astype(bf16)


def qkv_back_call(x, dx1, dq, dk, dv, gain, w):
    rows = x.shape[0]
    blk = 256
    block = pl.BlockSpec((blk, D), lambda i: (i, 0))
    return pl.pallas_call(
        qkv_back_body,
        name="qkv_back",
        grid=(rows // blk,),
        in_specs=[block, block, block, block, block, fixed((8, D)), fixed((D, 3 * D))],
        out_specs=[block, pl.BlockSpec((8, D), lambda i: (0, 0))],
        out_shape=[jax.ShapeDtypeStruct((rows, D), bf16), jax.ShapeDtypeStruct((8, D), f32)],
        compiler_params=params("arbitrary"),
        cost_estimate=pl.CostEstimate(
            flops=2 * rows * D * 3 * D, bytes_accessed=rows * D * 14, transcendentals=0
        ),
    )(x, dx1, dq, dk, dv, gain, w)


def qkv_grad_body(a1_ref, dq_ref, dk_ref, dv_ref, out_ref, acc_ref):
    step = pl.program_id(0)

    @pl.when(step == 0)
    def _():
        acc_ref[...] = jnp.zeros_like(acc_ref)

    a1 = a1_ref[...]
    for part, ref in enumerate((dq_ref, dk_ref, dv_ref)):
        acc_ref[:, part * D : (part + 1) * D] += mm(a1, ref[...], TN)

    @pl.when(step == pl.num_programs(0) - 1)
    def _():
        out_ref[...] = acc_ref[...].astype(bf16)


def qkv_grad_call(a1, dq, dk, dv):
    rows = a1.shape[0]
    blk = 512
    block = pl.BlockSpec((blk, D), lambda i: (i, 0))
    return pl.pallas_call(
        qkv_grad_body,
        name="qkv_grad",
        grid=(rows // blk,),
        in_specs=[block, block, block, block],
        out_specs=pl.BlockSpec((D, 3 * D), lambda i: (0, 0)),
        out_shape=jax.ShapeDtypeStruct((D, 3 * D), bf16),
        scratch_shapes=[pltpu.VMEM((D, 3 * D), f32)],
        compiler_params=params("arbitrary"),
        cost_estimate=pl.CostEstimate(
            flops=2 * rows * D * 3 * D, bytes_accessed=rows * D * 8, transcendentals=0
        ),
    )(a1, dq, dk, dv)


def feature_angles(time_steps, width):
    half = width // 2
    frequency = jnp.exp(jnp.arange(half, dtype=f32) * (-math.log(10000.0) / half))
    return time_steps.astype(f32)[:, None] * frequency[None, :]


def time_features(time_steps, width):
    angles = feature_angles(time_steps, width)
    return jnp.concatenate([jnp.cos(angles), jnp.sin(angles)], axis=-1).astype(bf16)


def row_tables(seq_spans):
    row = jnp.arange(BIN, dtype=jnp.int32)[None, :, None]
    spans = seq_spans.reshape(MB, 1, SLOTS, 2)
    offset = row - spans[..., 0]
    member = (offset >= 0) & (offset < spans[..., 1])
    position = jnp.sum(jnp.where(member, offset, 0), axis=2).astype(f32).reshape(ROWS, 1)
    lane = jnp.arange(LANES, dtype=jnp.int32)[None, :]
    half = HEAD // 2
    frequency = jnp.exp((lane % half).astype(f32) * (-math.log(10000.0) / half))
    angle = position * frequency
    cosine = jnp.cos(angle)
    sine = jnp.sin(angle) * jnp.where(lane % HEAD < half, -1.0, 1.0)
    member = member.reshape(ROWS, SLOTS)
    slot = jnp.arange(LANES, dtype=jnp.int32)[None, :]
    mine = jnp.sum(jnp.where((slot[:, None, :] == jnp.arange(SLOTS)[None, :, None]), member[:, :, None], False), axis=1)
    query_mask = jnp.where(mine > 0, neg_big, 0.0).astype(bf16)
    key_mask = jnp.where((mine == 0) & (slot < SLOTS), 1.0, 0.0).astype(bf16)
    return cosine, sine, query_mask, key_mask


def page_plan(page_deal, pages_dev, shards, device):
    per_peer = pages_dev // shards
    ids = jnp.arange(pages_dev, dtype=jnp.int32)
    deal = lax.dynamic_slice_in_dim(page_deal, device * pages_dev, pages_dev)
    target = deal // pages_dev
    earlier = (target[:, None] == target[None, :]) & (deal[None, :] < deal[:, None])
    send_pos = target * per_peer + jnp.sum(earlier.astype(jnp.int32), axis=1)
    send_order = jnp.sum(jnp.where(send_pos[None, :] == ids[:, None], ids[None, :], 0), axis=1)
    all_ids = jnp.arange(page_deal.shape[0], dtype=jnp.int32)
    hit = page_deal[None, :] == (device * pages_dev + ids)[:, None]
    owned = jnp.sum(jnp.where(hit, all_ids[None, :], 0), axis=1)
    source = owned // pages_dev
    before = (source[:, None] == source[None, :]) & (ids[None, :] < ids[:, None])
    recv_pos = source * per_peer + jnp.sum(before.astype(jnp.int32), axis=1)
    recv_order = jnp.sum(jnp.where(recv_pos[None, :] == ids[:, None], ids[None, :], 0), axis=1)
    return send_pos, send_order, recv_pos, recv_order


def pages(values):
    return values.reshape(-1, PAGE, D)


def exchange(values, shards):
    sent = values.reshape(shards, -1, PAGE, D)
    got = lax.all_to_all(sent, AXES, split_axis=0, concat_axis=0, tiled=True)
    return got.reshape(-1, PAGE, D)


def per_device(
    x_given, cotangent, norm_gain, w_qkv, w_out, w_ada, w_up, w_down, seq_spans, time_steps, page_deal
):
    shards = lax.axis_size(AXES)
    device = lax.axis_index(AXES)
    rows_dev = x_given.shape[0]
    pages_dev = rows_dev // PAGE
    send_pos, send_order, recv_pos, recv_order = page_plan(page_deal, pages_dev, shards, device)
    own = norm_gain.shape[0]
    parts = FF // D
    x_got = exchange(pages(x_given)[send_order], shards)
    dy_sent, x_got = lax.optimization_barrier((pages(cotangent)[send_order], x_got))
    dy_got = exchange(dy_sent, shards)
    x = x_got[recv_pos].reshape(rows_dev, D)

    def gather(*ws):
        return lax.all_gather(jnp.concatenate(ws, axis=1), AXES, axis=0, tiled=True)

    def reduce(g):
        return lax.optimization_barrier(lax.psum_scatter(g, AXES, scatter_dimension=0, tiled=True))

    up_own = w_up.reshape(own, shards, parts, own).transpose(0, 2, 1, 3).reshape(own, FF)
    down_own = w_down.reshape(parts, own, D).transpose(1, 0, 2).reshape(own, FF)
    first_all = gather(w_qkv, w_ada, jnp.broadcast_to(norm_gain[:, None], (own, LANES)))
    second_all = gather(up_own, down_own, w_out)
    ada_all = first_all[:, 3 * D : 6 * D]
    gain = jnp.broadcast_to(first_all[:, 6 * D].astype(f32)[None, :], (8, D))

    cosine, sine, query_mask, key_mask = row_tables(seq_spans)
    time_feat = time_features(time_steps, D)
    ada_seq = jnp.dot(time_feat, ada_all, preferred_element_type=f32)
    ada_seq = jnp.concatenate([ada_seq, jnp.zeros_like(ada_seq)], axis=0)
    feat = jnp.concatenate([time_feat, jnp.zeros_like(time_feat)], axis=0)
    feat = jnp.concatenate([feat, feat], axis=0)

    qkv, a1 = qkv_call(x, gain, first_all, cosine, sine)
    p, o, rl = attend_call(qkv, query_mask, key_mask)
    dy_got, o = lax.optimization_barrier((dy_got, o))
    dy = dy_got[recv_pos].reshape(rows_dev, D)
    y, dx1, do, grads = rows_call(seq_spans, x, o, dy, ada_seq, feat, second_all)

    y_sent, do = lax.optimization_barrier((pages(y)[recv_order], do))
    y_got = exchange(y_sent, shards)
    grads = reduce(grads)

    dq, dk, dv = attend_back_call(qkv, do, o, rl, p, cosine, sine)
    dq, y_got = lax.optimization_barrier((dq, y_got))
    dx, gg = qkv_back_call(x, dx1, dq, dk, dv, gain, first_all)
    dx_sent = pages(dx)[recv_order]
    output = y_got[send_pos].reshape(rows_dev, D)
    gq = qkv_grad_call(a1, dq, dk, dv)
    gq = jnp.concatenate([gq, jnp.broadcast_to(gg[0].astype(bf16)[:, None], (D, GAIN_COLS))], axis=1)
    gq, grads = lax.optimization_barrier((gq, grads))
    gq = reduce(gq)
    input_grad = exchange(dx_sent, shards)[send_pos].reshape(rows_dev, D)
    up_grad = grads[:, :FF].reshape(own, parts, shards, own).transpose(0, 2, 1, 3).reshape(own, FF)
    down_grad = grads[:, FF : 2 * FF].reshape(own, parts, D).transpose(1, 0, 2).reshape(parts * own, D)
    return (
        output,
        input_grad,
        gq[:, 3 * D].astype(f32),
        gq[:, : 3 * D].astype(f32),
        grads[:, 2 * FF : 2 * FF + D].astype(f32),
        grads[:, 2 * FF + D :].astype(f32),
        up_grad.astype(f32),
        down_grad.astype(f32),
    )


def solution(mesh):
    placed = P(AXES, None)
    vector = P(AXES)
    return jax.shard_map(
        per_device,
        mesh=mesh,
        in_specs=(placed, placed, vector, placed, placed, placed, placed, placed, placed, vector, P()),
        out_specs=(placed, placed, vector, placed, placed, placed, placed, placed),
        check_vma=False,
    )
```

```python
import functools
import math

import jax
import jax.numpy as jnp
from jax import lax
from jax.experimental import pallas as pl
from jax.experimental.pallas import tpu as pltpu
from jax.sharding import PartitionSpec as P

D = 768
HEADS = 12
HEAD = 64
FF = 3072
BIN = 1024
MB = 2
SLOTS = 2
PAGE = 16
LANES = 128
GAIN_COLS = 128
OUT_AT = 6 * D
GAIN_AT = 7 * D
UP_AT = 8 * D
PAIRS = HEADS // 2
ROWS = MB * BIN
CHUNK = 768
PIECE = 256
BLOCK = 256
VMEM_LIMIT = 60 << 20

eps = 1e-05
neg_big = -1e30
AXES = ("dp", "fsdp")
f32 = jnp.float32
bf16 = jnp.bfloat16

NN = (((1,), (0,)), ((), ()))
NT = (((1,), (1,)), ((), ()))
TN = (((0,), (0,)), ((), ()))


def mm(a, b, dims):
    return lax.dot_general(a, b, dims, preferred_element_type=f32)


def params(*semantics):
    return pltpu.CompilerParams(dimension_semantics=semantics, vmem_limit_bytes=VMEM_LIMIT)


def fixed(shape):
    return pl.BlockSpec(shape, lambda *g: (0,) * len(shape), pipeline_mode=pl.Buffered(1))


def normalise(values):
    center = jnp.mean(values, axis=-1, keepdims=True)
    shifted = values - center
    spread = jnp.mean(shifted * shifted, axis=-1, keepdims=True)
    inv = lax.rsqrt(spread + eps)
    return shifted * inv, inv


def partner(tile):
    lane = lax.broadcasted_iota(jnp.int32, tile.shape, 1)
    ahead = pltpu.roll(tile, LANES - HEAD // 2, 1)
    behind = pltpu.roll(tile, HEAD // 2, 1)
    return jnp.where(lane % HEAD < HEAD // 2, ahead, behind)


def qkv_body(x_ref, gain_ref, w_ref, cos_ref, sin_ref, qkv_ref, a1_ref):
    xhat, _ = normalise(x_ref[...].astype(f32))
    a1 = (xhat * gain_ref[0:1, :]).astype(bf16)
    a1_ref[...] = a1
    cosine, sine = cos_ref[...], sin_ref[...]
    for part in range(3):
        u = mm(a1, w_ref[:, part * D : (part + 1) * D], NN)
        for t in range(D // LANES):
            tile = u[:, t * LANES : (t + 1) * LANES]
            if part < 2:
                tile = tile * cosine + partner(tile) * sine
            if part == 0:
                tile = tile * 0.125
            at = part * D + t * LANES
            qkv_ref[:, at : at + LANES] = tile.astype(bf16)


def qkv_call(x, gain, w, cosine, sine):
    rows = x.shape[0]
    blk = 256
    return pl.pallas_call(
        qkv_body,
        name="qkv",
        grid=(rows // blk,),
        in_specs=[
            pl.BlockSpec((blk, D), lambda i: (i, 0)),
            fixed((8, D)),
            fixed((D, 3 * D)),
            pl.BlockSpec((blk, LANES), lambda i: (i, 0)),
            pl.BlockSpec((blk, LANES), lambda i: (i, 0)),
        ],
        out_specs=[
            pl.BlockSpec((blk, 3 * D), lambda i: (i, 0)),
            pl.BlockSpec((blk, D), lambda i: (i, 0)),
        ],
        out_shape=[
            jax.ShapeDtypeStruct((rows, 3 * D), bf16),
            jax.ShapeDtypeStruct((rows, D), bf16),
        ],
        compiler_params=params("arbitrary"),
        cost_estimate=pl.CostEstimate(
            flops=2 * rows * D * 3 * D, bytes_accessed=rows * D * 10, transcendentals=0
        ),
    )(x, gain, w, cosine, sine)


def attend_body(q_ref, k_ref, v_ref, qa_ref, ka_ref, p_ref, o_ref, rl_ref):
    pair = pl.program_id(1)
    blk = 256

    @pl.when(pair == 0)
    def _():
        rl_ref[...] = jnp.zeros_like(rl_ref)

    keys = jnp.concatenate([k_ref[...], ka_ref[...]], axis=1)
    vals = jnp.concatenate([v_ref[...], jnp.ones((BIN, LANES), bf16)], axis=1)
    lane = lax.broadcasted_iota(jnp.int32, (blk, LANES), 1)
    for rb in range(BIN // blk):
        rows = pl.ds(rb * blk, blk)
        q = q_ref[rows, :]
        outs = []
        for h in range(2):
            mine = (lane >= HEAD) == (h == 1)
            qh = jnp.concatenate([jnp.where(mine, q, jnp.zeros_like(q)), qa_ref[rows, :]], axis=1)
            s = mm(qh, keys, NT)
            top = jnp.max(s, axis=1, keepdims=True)
            p = jnp.exp(s - top).astype(bf16)
            p_ref[0, h, rows, :] = p
            ol = mm(p, vals, NN)
            rl = 1.0 / ol[:, LANES:]
            outs.append(ol[:, :LANES] * rl)
            rl_ref[rows, :] = jnp.where(lane == 2 * pair + h, rl, rl_ref[rows, :])
        o_ref[rows, :] = jnp.where(lane < HEAD, outs[0], outs[1]).astype(bf16)


def attend_call(qkv, qa, ka):
    bins = qkv.shape[0] // BIN
    tile = (BIN, LANES)
    return pl.pallas_call(
        attend_body,
        name="attend",
        grid=(bins, PAIRS),
        in_specs=[
            pl.BlockSpec(tile, lambda b, p: (b, p)),
            pl.BlockSpec(tile, lambda b, p: (b, PAIRS + p)),
            pl.BlockSpec(tile, lambda b, p: (b, 2 * PAIRS + p)),
            pl.BlockSpec(tile, lambda b, p: (b, 0)),
            pl.BlockSpec(tile, lambda b, p: (b, 0)),
        ],
        out_specs=[
            pl.BlockSpec((1, 2, BIN, BIN), lambda b, p: (b, p, 0, 0)),
            pl.BlockSpec(tile, lambda b, p: (b, p)),
            pl.BlockSpec(tile, lambda b, p: (b, 0)),
        ],
        out_shape=[
            jax.ShapeDtypeStruct((bins, HEADS, BIN, BIN), bf16),
            jax.ShapeDtypeStruct((bins * BIN, D), bf16),
            jax.ShapeDtypeStruct((bins * BIN, LANES), f32),
        ],
        compiler_params=params("arbitrary", "arbitrary"),
        cost_estimate=pl.CostEstimate(
            flops=bins * HEADS * BIN * BIN * 1024,
            bytes_accessed=bins * HEADS * BIN * BIN * 2,
            transcendentals=bins * HEADS * BIN * BIN,
        ),
    )(qkv, qkv, qkv, qa, ka)


def attend_back_body(
    q_ref, k_ref, v_ref, do_ref, o_ref, rl_ref, p_ref, cos_ref, sin_ref, dq_ref, dk_ref, dv_ref,
    dq_acc, dkt_acc, dvt_acc,
):
    pair = pl.program_id(1)
    blk = 256
    lane = lax.broadcasted_iota(jnp.int32, (blk, LANES), 1)
    lane_full = lax.broadcasted_iota(jnp.int32, (BIN, LANES), 1)

    def head(h, carry):
        vals = jnp.concatenate([v_ref[...], jnp.where(lane_full < 3, 1.0, 0.0).astype(bf16)], axis=1)
        mine = (lane >= HEAD) == (h == 1)
        dkt = jnp.zeros((LANES, BIN), f32)
        dvt = jnp.zeros((LANES, BIN), f32)
        for rb in range(BIN // blk):
            rows = pl.ds(rb * blk, blk)
            rl = jnp.sum(jnp.where(lane == 2 * pair + h, rl_ref[rows, :], 0.0), axis=1, keepdims=True)
            do = jnp.where(mine, do_ref[rows, :].astype(f32) * rl, 0.0).astype(bf16)
            delta = jnp.sum(do.astype(f32) * o_ref[rows, :].astype(f32), axis=1, keepdims=True)
            high = delta.astype(bf16).astype(f32)
            rest = delta - high
            mid = rest.astype(bf16).astype(f32)
            extra = jnp.where(lane == 0, -high, jnp.where(lane == 1, -mid, jnp.where(lane == 2, mid - rest, 0.0)))
            dp = mm(jnp.concatenate([do, extra.astype(bf16)], axis=1), vals, NT)
            p = p_ref[0, h, rows, :]
            ds = (p.astype(f32) * dp).astype(bf16)
            dq_acc[h, rows, :] = mm(ds, k_ref[...], NN)
            dkt += mm(q_ref[rows, :], ds, TN)
            dvt += mm(do, p, TN)
        dkt_acc[h] = dkt
        dvt_acc[h] = dvt
        return carry

    lax.fori_loop(0, 2, head, 0)
    sub = lax.broadcasted_iota(jnp.int32, (LANES, BIN), 0)
    dk = jnp.where(sub < HEAD, dkt_acc[0], dkt_acc[1]).T
    dv = jnp.where(sub < HEAD, dvt_acc[0], dvt_acc[1]).T
    cosine, sine = cos_ref[...], sin_ref[...]
    dq = jnp.where(lane_full < HEAD, dq_acc[0], dq_acc[1]) * 0.125
    dq_ref[...] = (dq * cosine - partner(dq) * sine).astype(bf16)
    dk_ref[...] = (dk * cosine - partner(dk) * sine).astype(bf16)
    dv_ref[...] = dv.astype(bf16)


def attend_back_call(qkv, do, o, rl, p, cosine, sine):
    bins = qkv.shape[0] // BIN
    tile = (BIN, LANES)
    grad = jax.ShapeDtypeStruct((bins * BIN, D), bf16)
    by_pair = pl.BlockSpec(tile, lambda b, p: (b, p))
    by_bin = pl.BlockSpec(tile, lambda b, p: (b, 0))
    return pl.pallas_call(
        attend_back_body,
        name="attend_back",
        grid=(bins, PAIRS),
        in_specs=[
            by_pair,
            pl.BlockSpec(tile, lambda b, p: (b, PAIRS + p)),
            pl.BlockSpec(tile, lambda b, p: (b, 2 * PAIRS + p)),
            by_pair,
            by_pair,
            by_bin,
            pl.BlockSpec((1, 2, BIN, BIN), lambda b, p: (b, p, 0, 0)),
            by_bin,
            by_bin,
        ],
        out_specs=[by_pair, by_pair, by_pair],
        out_shape=[grad, grad, grad],
        scratch_shapes=[
            pltpu.VMEM((2, BIN, LANES), f32),
            pltpu.VMEM((2, LANES, BIN), f32),
            pltpu.VMEM((2, LANES, BIN), f32),
        ],
        compiler_params=params("arbitrary", "arbitrary"),
        cost_estimate=pl.CostEstimate(
            flops=bins * HEADS * BIN * BIN * 2048,
            bytes_accessed=bins * HEADS * BIN * BIN * 2,
            transcendentals=0,
        ),
    )(qkv, qkv, qkv, do, o, rl, p, cosine, sine)


def rows_body(
    spans_ref, x_ref, o_ref, dy_ref, ada_ref, feat_ref, wo_ref, wu_ref, wd_ref,
    y_ref, dx1_ref, do_ref, grads_hbm,
    go_acc, gu_acc, gd_acc, dada_ref, hb_ref, dmlp_ref, mlp_ref, dh_ref, stage_ref, sem,
):
    step = pl.program_id(0)
    last = pl.num_programs(0) - 1
    here = step // (BIN // BLOCK)
    first_row = (step % (BIN // BLOCK)) * BLOCK

    @pl.when(step == 0)
    def _():
        go_acc[...] = jnp.zeros_like(go_acc)
        gu_acc[...] = jnp.zeros_like(gu_acc)
        gd_acc[...] = jnp.zeros_like(gd_acc)
        dada_ref[...] = jnp.zeros_like(dada_ref)

    row = lax.broadcasted_iota(jnp.int32, (BLOCK, 1), 0) + first_row
    owned = []
    for k in range(SLOTS):
        start = spans_ref[here * SLOTS + k, 0]
        length = spans_ref[here * SLOTS + k, 1]
        owned.append(jnp.where((row >= start) & (row < start + length), 1.0, 0.0).astype(f32))
    live = owned[0] + owned[1]

    def ada(part):
        cols = slice(part * D, (part + 1) * D)
        return sum(owned[k] * ada_ref[pl.ds(here * SLOTS + k, 1), cols] for k in range(SLOTS))

    def add_slots(part, values):
        cols = slice(part * D, (part + 1) * D)
        for k in range(SLOTS):
            at = pl.ds(here * SLOTS + k, 1)
            dada_ref[at, cols] += jnp.sum(owned[k] * values, axis=0, keepdims=True)

    o = o_ref[...]
    x1 = x_ref[...].astype(f32) + mm(o, wo_ref[...], NN)
    xhat, inv = normalise(x1)
    one_scale = 1.0 + ada(0)
    hb_ref[...] = (xhat * one_scale + ada(1)).astype(bf16)
    gate = ada(2)
    dy = live * dy_ref[...].astype(f32)
    dmlp_ref[...] = (dy * gate).astype(bf16)
    mlp_ref[...] = jnp.zeros_like(mlp_ref)
    dh_ref[...] = jnp.zeros_like(dh_ref)
    c0 = math.sqrt(2.0 / math.pi)

    def chunk(c, carry):
        cols = pl.ds(pl.multiple_of(c * CHUNK, CHUNK), CHUNK)
        u = mm(hb_ref[...], wu_ref[:, cols], NN)
        uu = u * u
        t = jnp.tanh(u * (c0 + (c0 * 0.044715) * uu))
        half = 0.5 + 0.5 * t
        gb = (u * half).astype(bf16)
        mlp_ref[...] += mm(gb, wd_ref[:, cols], NN)
        gd_acc[:, cols] += mm(gb, dmlp_ref[...], TN)
        slope = half + (u * (1.0 - t * t)) * (0.5 * c0 + (1.5 * c0 * 0.044715) * uu)
        du = (mm(dmlp_ref[...], wd_ref[:, cols], NT) * slope).astype(bf16)
        dh_ref[...] += mm(du, wu_ref[:, cols], NT)
        gu_acc[:, cols] += mm(hb_ref[...], du, TN)
        return carry

    lax.fori_loop(0, FF // CHUNK, chunk, 0)
    mlp, dh = mlp_ref[...], dh_ref[...]
    y_ref[...] = (live * (x1 + gate * mlp)).astype(bf16)
    add_slots(2, dy * mlp)
    add_slots(1, dh)
    add_slots(0, dh * xhat)
    e = dh * one_scale
    dx1 = dy + (e - jnp.mean(e, axis=1, keepdims=True) - xhat * jnp.mean(e * xhat, axis=1, keepdims=True)) * inv
    dx1_ref[...] = dx1
    dattn = dx1.astype(bf16)
    go_acc[...] += mm(o, dattn, TN)
    do_ref[...] = mm(dattn, wo_ref[...], NT).astype(bf16)

    @pl.when(step == last)
    def _():
        high = dada_ref[...].astype(bf16)
        low = (dada_ref[...] - high.astype(f32)).astype(bf16)
        sums = jnp.concatenate([high, low], axis=0)

        def slots_grad(r, c):
            return mm(feat_ref[:, r : r + PIECE], sums[:, c : c + D], TN)

        def held(acc):
            return lambda r, c: acc[r : r + PIECE, c : c + D]

        pieces = []
        for piece, first, width in (
            (held(gu_acc), 0, FF),
            (held(gd_acc), FF, FF),
            (held(go_acc), 2 * FF, D),
            (slots_grad, 2 * FF + D, 3 * D),
        ):
            for r in range(0, D, PIECE):
                for c in range(0, width, D):
                    pieces.append((piece, r, c, grads_hbm.at[r : r + PIECE, first + c : first + c + D]))
        copies = [None, None]
        for i, (piece, r, c, out) in enumerate(pieces):
            slot = i % 2
            if copies[slot] is not None:
                copies[slot].wait()
            stage_ref[slot] = piece(r, c).astype(bf16)
            copies[slot] = pltpu.make_async_copy(stage_ref.at[slot], out, sem.at[slot])
            copies[slot].start()
        for copy in copies:
            copy.wait()


def columns(width, index):
    return pl.BlockSpec((D, width), lambda *g: (0, index), pipeline_mode=pl.Buffered(1))


def rows_call(spans, x, o, dy, ada, feat, weights):
    rows = x.shape[0]
    block = pl.BlockSpec((BLOCK, D), lambda i, s: (i, 0))
    anywhere = pl.BlockSpec(memory_space=pl.ANY)
    return pl.pallas_call(
        rows_body,
        name="rows",
        grid_spec=pltpu.PrefetchScalarGridSpec(
            num_scalar_prefetch=1,
            grid=(rows // BLOCK,),
            in_specs=[
                block, block, block, fixed((8, 3 * D)), fixed((16, D)),
                columns(D, OUT_AT // D), columns(FF, UP_AT // FF), columns(FF, UP_AT // FF + 1),
            ],
            out_specs=[
                block, block, block, anywhere,
            ],
            scratch_shapes=[
                pltpu.VMEM((D, D), f32),
                pltpu.VMEM((D, FF), f32),
                pltpu.VMEM((D, FF), f32),
                pltpu.VMEM((8, 3 * D), f32),
                pltpu.VMEM((BLOCK, D), bf16),
                pltpu.VMEM((BLOCK, D), bf16),
                pltpu.VMEM((BLOCK, D), f32),
                pltpu.VMEM((BLOCK, D), f32),
                pltpu.VMEM((2, PIECE, D), bf16),
                pltpu.SemaphoreType.DMA((2,)),
            ],
        ),
        out_shape=[
            jax.ShapeDtypeStruct((rows, D), bf16),
            jax.ShapeDtypeStruct((rows, D), f32),
            jax.ShapeDtypeStruct((rows, D), bf16),
            jax.ShapeDtypeStruct((D, 2 * FF + 4 * D), bf16),
        ],
        compiler_params=params("arbitrary"),
        cost_estimate=pl.CostEstimate(
            flops=6 * rows * D * (D + 2 * FF), bytes_accessed=rows * D * 14, transcendentals=rows * FF
        ),
    )(spans, x, o, dy, ada, feat, weights, weights, weights)


def qkv_back_body(x_ref, dx1_ref, dq_ref, dk_ref, dv_ref, gain_ref, w_ref, dx_ref, gg_ref):
    @pl.when(pl.program_id(0) == 0)
    def _():
        gg_ref[...] = jnp.zeros_like(gg_ref)

    xhat, inv = normalise(x_ref[...].astype(f32))
    dn = mm(dq_ref[...], w_ref[:, :D], NT)
    dn += mm(dk_ref[...], w_ref[:, D : 2 * D], NT)
    dn += mm(dv_ref[...], w_ref[:, 2 * D :], NT)
    gg_ref[0:1, :] += jnp.sum(dn * xhat, axis=0, keepdims=True)
    e = dn * gain_ref[0:1, :]
    back = (e - jnp.mean(e, axis=1, keepdims=True) - xhat * jnp.mean(e * xhat, axis=1, keepdims=True)) * inv
    dx_ref[...] = (dx1_ref[...] + back).astype(bf16)


def qkv_back_call(x, dx1, dq, dk, dv, gain, w):
    rows = x.shape[0]
    blk = 256
    block = pl.BlockSpec((blk, D), lambda i: (i, 0))
    return pl.pallas_call(
        qkv_back_body,
        name="qkv_back",
        grid=(rows // blk,),
        in_specs=[block, block, block, block, block, fixed((8, D)), fixed((D, 3 * D))],
        out_specs=[block, pl.BlockSpec((8, D), lambda i: (0, 0))],
        out_shape=[jax.ShapeDtypeStruct((rows, D), bf16), jax.ShapeDtypeStruct((8, D), f32)],
        compiler_params=params("arbitrary"),
        cost_estimate=pl.CostEstimate(
            flops=2 * rows * D * 3 * D, bytes_accessed=rows * D * 14, transcendentals=0
        ),
    )(x, dx1, dq, dk, dv, gain, w)


def qkv_grad_body(a1_ref, dq_ref, dk_ref, dv_ref, out_ref, acc_ref):
    step = pl.program_id(0)

    @pl.when(step == 0)
    def _():
        acc_ref[...] = jnp.zeros_like(acc_ref)

    a1 = a1_ref[...]
    for part, ref in enumerate((dq_ref, dk_ref, dv_ref)):
        acc_ref[:, part * D : (part + 1) * D] += mm(a1, ref[...], TN)

    @pl.when(step == pl.num_programs(0) - 1)
    def _():
        out_ref[...] = acc_ref[...].astype(bf16)


def qkv_grad_call(a1, dq, dk, dv):
    rows = a1.shape[0]
    blk = 512
    block = pl.BlockSpec((blk, D), lambda i: (i, 0))
    return pl.pallas_call(
        qkv_grad_body,
        name="qkv_grad",
        grid=(rows // blk,),
        in_specs=[block, block, block, block],
        out_specs=pl.BlockSpec((D, 3 * D), lambda i: (0, 0)),
        out_shape=jax.ShapeDtypeStruct((D, 3 * D), bf16),
        scratch_shapes=[pltpu.VMEM((D, 3 * D), f32)],
        compiler_params=params("arbitrary"),
        cost_estimate=pl.CostEstimate(
            flops=2 * rows * D * 3 * D, bytes_accessed=rows * D * 8, transcendentals=0
        ),
    )(a1, dq, dk, dv)


def feature_angles(time_steps, width):
    half = width // 2
    frequency = jnp.exp(jnp.arange(half, dtype=f32) * (-math.log(10000.0) / half))
    return time_steps.astype(f32)[:, None] * frequency[None, :]


def time_features(time_steps, width):
    angles = feature_angles(time_steps, width)
    return jnp.concatenate([jnp.cos(angles), jnp.sin(angles)], axis=-1).astype(bf16)


def row_tables(seq_spans):
    row = jnp.arange(BIN, dtype=jnp.int32)[None, :, None]
    spans = seq_spans.reshape(MB, 1, SLOTS, 2)
    offset = row - spans[..., 0]
    member = (offset >= 0) & (offset < spans[..., 1])
    position = jnp.sum(jnp.where(member, offset, 0), axis=2).astype(f32).reshape(ROWS, 1)
    lane = jnp.arange(LANES, dtype=jnp.int32)[None, :]
    half = HEAD // 2
    frequency = jnp.exp((lane % half).astype(f32) * (-math.log(10000.0) / half))
    angle = position * frequency
    cosine = jnp.cos(angle)
    sine = jnp.sin(angle) * jnp.where(lane % HEAD < half, -1.0, 1.0)
    member = member.reshape(ROWS, SLOTS)
    slot = jnp.arange(LANES, dtype=jnp.int32)[None, :]
    mine = jnp.sum(jnp.where((slot[:, None, :] == jnp.arange(SLOTS)[None, :, None]), member[:, :, None], False), axis=1)
    query_mask = jnp.where(mine > 0, neg_big, 0.0).astype(bf16)
    key_mask = jnp.where((mine == 0) & (slot < SLOTS), 1.0, 0.0).astype(bf16)
    return cosine, sine, query_mask, key_mask


def page_plan(page_deal, pages_dev, shards, device):
    per_peer = pages_dev // shards
    ids = jnp.arange(pages_dev, dtype=jnp.int32)
    deal = lax.dynamic_slice_in_dim(page_deal, device * pages_dev, pages_dev)
    target = deal // pages_dev
    earlier = (target[:, None] == target[None, :]) & (deal[None, :] < deal[:, None])
    send_pos = target * per_peer + jnp.sum(earlier.astype(jnp.int32), axis=1)
    send_order = jnp.sum(jnp.where(send_pos[None, :] == ids[:, None], ids[None, :], 0), axis=1)
    all_ids = jnp.arange(page_deal.shape[0], dtype=jnp.int32)
    hit = page_deal[None, :] == (device * pages_dev + ids)[:, None]
    owned = jnp.sum(jnp.where(hit, all_ids[None, :], 0), axis=1)
    source = owned // pages_dev
    before = (source[:, None] == source[None, :]) & (ids[None, :] < ids[:, None])
    recv_pos = source * per_peer + jnp.sum(before.astype(jnp.int32), axis=1)
    recv_order = jnp.sum(jnp.where(recv_pos[None, :] == ids[:, None], ids[None, :], 0), axis=1)
    return send_pos, send_order, recv_pos, recv_order


def pages(values):
    return values.reshape(-1, PAGE, D)


def exchange(values, shards):
    sent = values.reshape(shards, -1, PAGE, D)
    got = lax.all_to_all(sent, AXES, split_axis=0, concat_axis=0, tiled=True)
    return got.reshape(-1, PAGE, D)


def per_device(
    x_given, cotangent, norm_gain, w_qkv, w_out, w_ada, w_up, w_down, seq_spans, time_steps, page_deal
):
    shards = lax.axis_size(AXES)
    device = lax.axis_index(AXES)
    rows_dev = x_given.shape[0]
    pages_dev = rows_dev // PAGE
    send_pos, send_order, recv_pos, recv_order = page_plan(page_deal, pages_dev, shards, device)
    own = norm_gain.shape[0]
    parts = FF // D
    x_got = exchange(pages(x_given)[send_order], shards)
    dy_sent, x_got = lax.optimization_barrier((pages(cotangent)[send_order], x_got))
    dy_got = exchange(dy_sent, shards)
    x = x_got[recv_pos].reshape(rows_dev, D)

    def gather(*ws):
        return lax.all_gather(jnp.concatenate(ws, axis=1), AXES, axis=0, tiled=True)

    def reduce(g):
        return lax.optimization_barrier(lax.psum_scatter(g, AXES, scatter_dimension=0, tiled=True))

    up_own = w_up.reshape(own, shards, parts, own).transpose(0, 2, 1, 3).reshape(own, FF)
    down_own = w_down.reshape(parts, own, D).transpose(1, 0, 2).reshape(own, FF)
    gain_own = jnp.broadcast_to(norm_gain[:, None], (own, UP_AT - GAIN_AT))
    weights = gather(w_qkv, w_ada, w_out, gain_own, up_own, down_own)
    ada_all = weights[:, 3 * D : 6 * D]
    gain = jnp.broadcast_to(weights[:, GAIN_AT].astype(f32)[None, :], (8, D))

    cosine, sine, query_mask, key_mask = row_tables(seq_spans)
    time_feat = time_features(time_steps, D)
    ada_seq = jnp.dot(time_feat, ada_all, preferred_element_type=f32)
    ada_seq = jnp.concatenate([ada_seq, jnp.zeros_like(ada_seq)], axis=0)
    feat = jnp.concatenate([time_feat, jnp.zeros_like(time_feat)], axis=0)
    feat = jnp.concatenate([feat, feat], axis=0)

    qkv, a1 = qkv_call(x, gain, weights, cosine, sine)
    p, o, rl = attend_call(qkv, query_mask, key_mask)
    dy_got, o = lax.optimization_barrier((dy_got, o))
    dy = dy_got[recv_pos].reshape(rows_dev, D)
    y, dx1, do, grads = rows_call(seq_spans, x, o, dy, ada_seq, feat, weights)

    y_sent, do = lax.optimization_barrier((pages(y)[recv_order], do))
    y_got = exchange(y_sent, shards)
    grads = reduce(grads)

    dq, dk, dv = attend_back_call(qkv, do, o, rl, p, cosine, sine)
    dq, y_got = lax.optimization_barrier((dq, y_got))
    dx, gg = qkv_back_call(x, dx1, dq, dk, dv, gain, weights)
    dx_sent = pages(dx)[recv_order]
    output = y_got[send_pos].reshape(rows_dev, D)
    gq = qkv_grad_call(a1, dq, dk, dv)
    gq = jnp.concatenate([gq, jnp.broadcast_to(gg[0].astype(bf16)[:, None], (D, GAIN_COLS))], axis=1)
    gq, grads, dx_sent = lax.optimization_barrier((gq, grads, dx_sent))
    gq = reduce(gq)
    input_grad = exchange(dx_sent, shards)[send_pos].reshape(rows_dev, D)
    up_grad = grads[:, :FF].reshape(own, parts, shards, own).transpose(0, 2, 1, 3).reshape(own, FF)
    down_grad = grads[:, FF : 2 * FF].reshape(own, parts, D).transpose(1, 0, 2).reshape(parts * own, D)
    return (
        output,
        input_grad,
        gq[:, 3 * D].astype(f32),
        gq[:, : 3 * D].astype(f32),
        grads[:, 2 * FF : 2 * FF + D].astype(f32),
        grads[:, 2 * FF + D :].astype(f32),
        up_grad.astype(f32),
        down_grad.astype(f32),
    )


def solution(mesh):
    placed = P(AXES, None)
    vector = P(AXES)
    return jax.shard_map(
        per_device,
        mesh=mesh,
        in_specs=(placed, placed, vector, placed, placed, placed, placed, placed, placed, vector, P()),
        out_specs=(placed, placed, vector, placed, placed, placed, placed, placed),
        check_vma=False,
    )
```

```python
import functools
import math

import jax
import jax.numpy as jnp
from jax import lax
from jax.experimental import pallas as pl
from jax.experimental.pallas import tpu as pltpu
from jax.sharding import PartitionSpec as P

D = 768
HEADS = 12
HEAD = 64
FF = 3072
BIN = 1024
MB = 2
SLOTS = 2
PAGE = 16
LANES = 128
GAIN_COLS = 128
PAIRS = HEADS // 2
ROWS = MB * BIN
CHUNK = 768
PIECE = 256
BLOCK = 256
VMEM_LIMIT = 60 << 20

eps = 1e-05
neg_big = -1e30
AXES = ("dp", "fsdp")
f32 = jnp.float32
bf16 = jnp.bfloat16

NN = (((1,), (0,)), ((), ()))
NT = (((1,), (1,)), ((), ()))
TN = (((0,), (0,)), ((), ()))


def mm(a, b, dims):
    return lax.dot_general(a, b, dims, preferred_element_type=f32)


def params(*semantics):
    return pltpu.CompilerParams(dimension_semantics=semantics, vmem_limit_bytes=VMEM_LIMIT)


def fixed(shape):
    return pl.BlockSpec(shape, lambda *g: (0,) * len(shape), pipeline_mode=pl.Buffered(1))


def normalise(values):
    center = jnp.mean(values, axis=-1, keepdims=True)
    shifted = values - center
    spread = jnp.mean(shifted * shifted, axis=-1, keepdims=True)
    inv = lax.rsqrt(spread + eps)
    return shifted * inv, inv


def partner(tile):
    lane = lax.broadcasted_iota(jnp.int32, tile.shape, 1)
    ahead = pltpu.roll(tile, LANES - HEAD // 2, 1)
    behind = pltpu.roll(tile, HEAD // 2, 1)
    return jnp.where(lane % HEAD < HEAD // 2, ahead, behind)


def qkv_body(x_ref, gain_ref, w_ref, cos_ref, sin_ref, qkv_ref, a1_ref):
    xhat, _ = normalise(x_ref[...].astype(f32))
    a1 = (xhat * gain_ref[0:1, :]).astype(bf16)
    a1_ref[...] = a1
    cosine, sine = cos_ref[...], sin_ref[...]
    for part in range(3):
        u = mm(a1, w_ref[:, part * D : (part + 1) * D], NN)
        for t in range(D // LANES):
            tile = u[:, t * LANES : (t + 1) * LANES]
            if part < 2:
                tile = tile * cosine + partner(tile) * sine
            if part == 0:
                tile = tile * 0.125
            at = part * D + t * LANES
            qkv_ref[:, at : at + LANES] = tile.astype(bf16)


def qkv_call(x, gain, w, cosine, sine):
    rows = x.shape[0]
    blk = 256
    return pl.pallas_call(
        qkv_body,
        name="qkv",
        grid=(rows // blk,),
        in_specs=[
            pl.BlockSpec((blk, D), lambda i: (i, 0)),
            fixed((8, D)),
            fixed((D, 3 * D)),
            pl.BlockSpec((blk, LANES), lambda i: (i, 0)),
            pl.BlockSpec((blk, LANES), lambda i: (i, 0)),
        ],
        out_specs=[
            pl.BlockSpec((blk, 3 * D), lambda i: (i, 0)),
            pl.BlockSpec((blk, D), lambda i: (i, 0)),
        ],
        out_shape=[
            jax.ShapeDtypeStruct((rows, 3 * D), bf16),
            jax.ShapeDtypeStruct((rows, D), bf16),
        ],
        compiler_params=params("arbitrary"),
        cost_estimate=pl.CostEstimate(
            flops=2 * rows * D * 3 * D, bytes_accessed=rows * D * 10, transcendentals=0
        ),
    )(x, gain, w, cosine, sine)


def attend_body(q_ref, k_ref, v_ref, qa_ref, ka_ref, p_ref, o_ref, rl_ref):
    pair = pl.program_id(1)
    blk = 256

    @pl.when(pair == 0)
    def _():
        rl_ref[...] = jnp.zeros_like(rl_ref)

    keys = jnp.concatenate([k_ref[...], ka_ref[...]], axis=1)
    vals = jnp.concatenate([v_ref[...], jnp.ones((BIN, LANES), bf16)], axis=1)
    lane = lax.broadcasted_iota(jnp.int32, (blk, LANES), 1)
    for rb in range(BIN // blk):
        rows = pl.ds(rb * blk, blk)
        q = q_ref[rows, :]
        outs = []
        for h in range(2):
            mine = (lane >= HEAD) == (h == 1)
            qh = jnp.concatenate([jnp.where(mine, q, jnp.zeros_like(q)), qa_ref[rows, :]], axis=1)
            s = mm(qh, keys, NT)
            top = jnp.max(s, axis=1, keepdims=True)
            p = jnp.exp(s - top).astype(bf16)
            p_ref[0, h, rows, :] = p
            ol = mm(p, vals, NN)
            rl = 1.0 / ol[:, LANES:]
            outs.append(ol[:, :LANES] * rl)
            rl_ref[rows, :] = jnp.where(lane == 2 * pair + h, rl, rl_ref[rows, :])
        o_ref[rows, :] = jnp.where(lane < HEAD, outs[0], outs[1]).astype(bf16)


def attend_call(qkv, qa, ka):
    bins = qkv.shape[0] // BIN
    tile = (BIN, LANES)
    return pl.pallas_call(
        attend_body,
        name="attend",
        grid=(bins, PAIRS),
        in_specs=[
            pl.BlockSpec(tile, lambda b, p: (b, p)),
            pl.BlockSpec(tile, lambda b, p: (b, PAIRS + p)),
            pl.BlockSpec(tile, lambda b, p: (b, 2 * PAIRS + p)),
            pl.BlockSpec(tile, lambda b, p: (b, 0)),
            pl.BlockSpec(tile, lambda b, p: (b, 0)),
        ],
        out_specs=[
            pl.BlockSpec((1, 2, BIN, BIN), lambda b, p: (b, p, 0, 0)),
            pl.BlockSpec(tile, lambda b, p: (b, p)),
            pl.BlockSpec(tile, lambda b, p: (b, 0)),
        ],
        out_shape=[
            jax.ShapeDtypeStruct((bins, HEADS, BIN, BIN), bf16),
            jax.ShapeDtypeStruct((bins * BIN, D), bf16),
            jax.ShapeDtypeStruct((bins * BIN, LANES), f32),
        ],
        compiler_params=params("arbitrary", "arbitrary"),
        cost_estimate=pl.CostEstimate(
            flops=bins * HEADS * BIN * BIN * 1024,
            bytes_accessed=bins * HEADS * BIN * BIN * 2,
            transcendentals=bins * HEADS * BIN * BIN,
        ),
    )(qkv, qkv, qkv, qa, ka)


def attend_back_body(
    q_ref, k_ref, v_ref, do_ref, o_ref, rl_ref, p_ref, cos_ref, sin_ref, dq_ref, dk_ref, dv_ref,
    dq_acc, dkt_acc, dvt_acc,
):
    pair = pl.program_id(1)
    blk = 256
    lane = lax.broadcasted_iota(jnp.int32, (blk, LANES), 1)
    lane_full = lax.broadcasted_iota(jnp.int32, (BIN, LANES), 1)

    def head(h, carry):
        vals = jnp.concatenate([v_ref[...], jnp.where(lane_full < 3, 1.0, 0.0).astype(bf16)], axis=1)
        mine = (lane >= HEAD) == (h == 1)
        dkt = jnp.zeros((LANES, BIN), f32)
        dvt = jnp.zeros((LANES, BIN), f32)
        for rb in range(BIN // blk):
            rows = pl.ds(rb * blk, blk)
            rl = jnp.sum(jnp.where(lane == 2 * pair + h, rl_ref[rows, :], 0.0), axis=1, keepdims=True)
            do = jnp.where(mine, do_ref[rows, :].astype(f32) * rl, 0.0).astype(bf16)
            delta = jnp.sum(do.astype(f32) * o_ref[rows, :].astype(f32), axis=1, keepdims=True)
            high = delta.astype(bf16).astype(f32)
            rest = delta - high
            mid = rest.astype(bf16).astype(f32)
            extra = jnp.where(lane == 0, -high, jnp.where(lane == 1, -mid, jnp.where(lane == 2, mid - rest, 0.0)))
            dp = mm(jnp.concatenate([do, extra.astype(bf16)], axis=1), vals, NT)
            p = p_ref[0, h, rows, :]
            ds = (p.astype(f32) * dp).astype(bf16)
            dq_acc[h, rows, :] = mm(ds, k_ref[...], NN)
            dkt += mm(q_ref[rows, :], ds, TN)
            dvt += mm(do, p, TN)
        dkt_acc[h] = dkt
        dvt_acc[h] = dvt
        return carry

    lax.fori_loop(0, 2, head, 0)
    sub = lax.broadcasted_iota(jnp.int32, (LANES, BIN), 0)
    dk = jnp.where(sub < HEAD, dkt_acc[0], dkt_acc[1]).T
    dv = jnp.where(sub < HEAD, dvt_acc[0], dvt_acc[1]).T
    cosine, sine = cos_ref[...], sin_ref[...]
    dq = jnp.where(lane_full < HEAD, dq_acc[0], dq_acc[1]) * 0.125
    dq_ref[...] = (dq * cosine - partner(dq) * sine).astype(bf16)
    dk_ref[...] = (dk * cosine - partner(dk) * sine).astype(bf16)
    dv_ref[...] = dv.astype(bf16)


def attend_back_call(qkv, do, o, rl, p, cosine, sine):
    bins = qkv.shape[0] // BIN
    tile = (BIN, LANES)
    grad = jax.ShapeDtypeStruct((bins * BIN, D), bf16)
    by_pair = pl.BlockSpec(tile, lambda b, p: (b, p))
    by_bin = pl.BlockSpec(tile, lambda b, p: (b, 0))
    return pl.pallas_call(
        attend_back_body,
        name="attend_back",
        grid=(bins, PAIRS),
        in_specs=[
            by_pair,
            pl.BlockSpec(tile, lambda b, p: (b, PAIRS + p)),
            pl.BlockSpec(tile, lambda b, p: (b, 2 * PAIRS + p)),
            by_pair,
            by_pair,
            by_bin,
            pl.BlockSpec((1, 2, BIN, BIN), lambda b, p: (b, p, 0, 0)),
            by_bin,
            by_bin,
        ],
        out_specs=[by_pair, by_pair, by_pair],
        out_shape=[grad, grad, grad],
        scratch_shapes=[
            pltpu.VMEM((2, BIN, LANES), f32),
            pltpu.VMEM((2, LANES, BIN), f32),
            pltpu.VMEM((2, LANES, BIN), f32),
        ],
        compiler_params=params("arbitrary", "arbitrary"),
        cost_estimate=pl.CostEstimate(
            flops=bins * HEADS * BIN * BIN * 2048,
            bytes_accessed=bins * HEADS * BIN * BIN * 2,
            transcendentals=0,
        ),
    )(qkv, qkv, qkv, do, o, rl, p, cosine, sine)


def rows_body(
    spans_ref, x_ref, o_ref, dy_ref, ada_ref, feat_ref, wo_ref, wu_ref, wd_ref,
    y_ref, dx1_ref, do_ref, grads_hbm,
    go_acc, gu_acc, gd_acc, dada_ref, hb_ref, dmlp_ref, mlp_ref, dh_ref, stage_ref, sem,
):
    step = pl.program_id(0)
    last = pl.num_programs(0) - 1
    here = step // (BIN // BLOCK)
    first_row = (step % (BIN // BLOCK)) * BLOCK

    @pl.when(step == 0)
    def _():
        go_acc[...] = jnp.zeros_like(go_acc)
        gu_acc[...] = jnp.zeros_like(gu_acc)
        gd_acc[...] = jnp.zeros_like(gd_acc)
        dada_ref[...] = jnp.zeros_like(dada_ref)

    row = lax.broadcasted_iota(jnp.int32, (BLOCK, 1), 0) + first_row
    owned = []
    for k in range(SLOTS):
        start = spans_ref[here * SLOTS + k, 0]
        length = spans_ref[here * SLOTS + k, 1]
        owned.append(jnp.where((row >= start) & (row < start + length), 1.0, 0.0).astype(f32))
    live = owned[0] + owned[1]

    def ada(part):
        cols = slice(part * D, (part + 1) * D)
        return sum(owned[k] * ada_ref[pl.ds(here * SLOTS + k, 1), cols] for k in range(SLOTS))

    def add_slots(part, values):
        cols = slice(part * D, (part + 1) * D)
        for k in range(SLOTS):
            at = pl.ds(here * SLOTS + k, 1)
            dada_ref[at, cols] += jnp.sum(owned[k] * values, axis=0, keepdims=True)

    o = o_ref[...]
    x1 = x_ref[...].astype(f32) + mm(o, wo_ref[...], NN)
    xhat, inv = normalise(x1)
    one_scale = 1.0 + ada(0)
    hb_ref[...] = (xhat * one_scale + ada(1)).astype(bf16)
    gate = ada(2)
    dy = live * dy_ref[...].astype(f32)
    dmlp_ref[...] = (dy * gate).astype(bf16)
    mlp_ref[...] = jnp.zeros_like(mlp_ref)
    dh_ref[...] = jnp.zeros_like(dh_ref)
    c0 = math.sqrt(2.0 / math.pi)

    def chunk(c, carry):
        cols = pl.ds(pl.multiple_of(c * CHUNK, CHUNK), CHUNK)
        u = mm(hb_ref[...], wu_ref[:, cols], NN)
        uu = u * u
        t = jnp.tanh(u * (c0 + (c0 * 0.044715) * uu))
        half = 0.5 + 0.5 * t
        gb = (u * half).astype(bf16)
        mlp_ref[...] += mm(gb, wd_ref[:, cols], NN)
        gd_acc[:, cols] += mm(gb, dmlp_ref[...], TN)
        slope = half + (u * (1.0 - t * t)) * (0.5 * c0 + (1.5 * c0 * 0.044715) * uu)
        du = (mm(dmlp_ref[...], wd_ref[:, cols], NT) * slope).astype(bf16)
        dh_ref[...] += mm(du, wu_ref[:, cols], NT)
        gu_acc[:, cols] += mm(hb_ref[...], du, TN)
        return carry

    lax.fori_loop(0, FF // CHUNK, chunk, 0)
    mlp, dh = mlp_ref[...], dh_ref[...]
    y_ref[...] = (live * (x1 + gate * mlp)).astype(bf16)
    add_slots(2, dy * mlp)
    add_slots(1, dh)
    add_slots(0, dh * xhat)
    e = dh * one_scale
    dx1 = dy + (e - jnp.mean(e, axis=1, keepdims=True) - xhat * jnp.mean(e * xhat, axis=1, keepdims=True)) * inv
    dx1_ref[...] = dx1
    dattn = dx1.astype(bf16)
    go_acc[...] += mm(o, dattn, TN)
    do_ref[...] = mm(dattn, wo_ref[...], NT).astype(bf16)

    @pl.when(step == last)
    def _():
        high = dada_ref[...].astype(bf16)
        low = (dada_ref[...] - high.astype(f32)).astype(bf16)
        sums = jnp.concatenate([high, low], axis=0)

        def slots_grad(r, c):
            return mm(feat_ref[:, r : r + PIECE], sums[:, c : c + D], TN)

        def held(acc):
            return lambda r, c: acc[r : r + PIECE, c : c + D]

        pieces = []
        for piece, first, width in (
            (held(gu_acc), 0, FF),
            (held(gd_acc), FF, FF),
            (held(go_acc), 2 * FF, D),
            (slots_grad, 2 * FF + D, 3 * D),
        ):
            for r in range(0, D, PIECE):
                for c in range(0, width, D):
                    pieces.append((piece, r, c, grads_hbm.at[r : r + PIECE, first + c : first + c + D]))
        copies = [None, None]
        for i, (piece, r, c, out) in enumerate(pieces):
            slot = i % 2
            if copies[slot] is not None:
                copies[slot].wait()
            stage_ref[slot] = piece(r, c).astype(bf16)
            copies[slot] = pltpu.make_async_copy(stage_ref.at[slot], out, sem.at[slot])
            copies[slot].start()
        for copy in copies:
            copy.wait()


def columns(width, index):
    return pl.BlockSpec((D, width), lambda *g: (0, index), pipeline_mode=pl.Buffered(1))


def rows_call(spans, x, o, dy, ada, feat, weights):
    rows = x.shape[0]
    block = pl.BlockSpec((BLOCK, D), lambda i, s: (i, 0))
    anywhere = pl.BlockSpec(memory_space=pl.ANY)
    return pl.pallas_call(
        rows_body,
        name="rows",
        grid_spec=pltpu.PrefetchScalarGridSpec(
            num_scalar_prefetch=1,
            grid=(rows // BLOCK,),
            in_specs=[
                block, block, block, fixed((8, 3 * D)), fixed((16, D)),
                columns(D, 2 * FF // D), columns(FF, 0), columns(FF, 1),
            ],
            out_specs=[
                block, block, block, anywhere,
            ],
            scratch_shapes=[
                pltpu.VMEM((D, D), f32),
                pltpu.VMEM((D, FF), f32),
                pltpu.VMEM((D, FF), f32),
                pltpu.VMEM((8, 3 * D), f32),
                pltpu.VMEM((BLOCK, D), bf16),
                pltpu.VMEM((BLOCK, D), bf16),
                pltpu.VMEM((BLOCK, D), f32),
                pltpu.VMEM((BLOCK, D), f32),
                pltpu.VMEM((2, PIECE, D), bf16),
                pltpu.SemaphoreType.DMA((2,)),
            ],
        ),
        out_shape=[
            jax.ShapeDtypeStruct((rows, D), bf16),
            jax.ShapeDtypeStruct((rows, D), f32),
            jax.ShapeDtypeStruct((rows, D), bf16),
            jax.ShapeDtypeStruct((D, 2 * FF + 4 * D), bf16),
        ],
        compiler_params=params("arbitrary"),
        cost_estimate=pl.CostEstimate(
            flops=6 * rows * D * (D + 2 * FF), bytes_accessed=rows * D * 14, transcendentals=rows * FF
        ),
    )(spans, x, o, dy, ada, feat, weights, weights, weights)


def qkv_back_body(x_ref, dx1_ref, dq_ref, dk_ref, dv_ref, gain_ref, w_ref, dx_ref, gg_ref):
    @pl.when(pl.program_id(0) == 0)
    def _():
        gg_ref[...] = jnp.zeros_like(gg_ref)

    xhat, inv = normalise(x_ref[...].astype(f32))
    dn = mm(dq_ref[...], w_ref[:, :D], NT)
    dn += mm(dk_ref[...], w_ref[:, D : 2 * D], NT)
    dn += mm(dv_ref[...], w_ref[:, 2 * D :], NT)
    gg_ref[0:1, :] += jnp.sum(dn * xhat, axis=0, keepdims=True)
    e = dn * gain_ref[0:1, :]
    back = (e - jnp.mean(e, axis=1, keepdims=True) - xhat * jnp.mean(e * xhat, axis=1, keepdims=True)) * inv
    dx_ref[...] = (dx1_ref[...] + back).astype(bf16)


def qkv_back_call(x, dx1, dq, dk, dv, gain, w):
    rows = x.shape[0]
    blk = 256
    block = pl.BlockSpec((blk, D), lambda i: (i, 0))
    return pl.pallas_call(
        qkv_back_body,
        name="qkv_back",
        grid=(rows // blk,),
        in_specs=[block, block, block, block, block, fixed((8, D)), fixed((D, 3 * D))],
        out_specs=[block, pl.BlockSpec((8, D), lambda i: (0, 0))],
        out_shape=[jax.ShapeDtypeStruct((rows, D), bf16), jax.ShapeDtypeStruct((8, D), f32)],
        compiler_params=params("arbitrary"),
        cost_estimate=pl.CostEstimate(
            flops=2 * rows * D * 3 * D, bytes_accessed=rows * D * 14, transcendentals=0
        ),
    )(x, dx1, dq, dk, dv, gain, w)


def qkv_grad_body(a1_ref, dq_ref, dk_ref, dv_ref, out_ref, acc_ref):
    step = pl.program_id(0)

    @pl.when(step == 0)
    def _():
        acc_ref[...] = jnp.zeros_like(acc_ref)

    a1 = a1_ref[...]
    for part, ref in enumerate((dq_ref, dk_ref, dv_ref)):
        acc_ref[:, part * D : (part + 1) * D] += mm(a1, ref[...], TN)

    @pl.when(step == pl.num_programs(0) - 1)
    def _():
        out_ref[...] = acc_ref[...].astype(bf16)


def qkv_grad_call(a1, dq, dk, dv):
    rows = a1.shape[0]
    blk = 512
    block = pl.BlockSpec((blk, D), lambda i: (i, 0))
    return pl.pallas_call(
        qkv_grad_body,
        name="qkv_grad",
        grid=(rows // blk,),
        in_specs=[block, block, block, block],
        out_specs=pl.BlockSpec((D, 3 * D), lambda i: (0, 0)),
        out_shape=jax.ShapeDtypeStruct((D, 3 * D), bf16),
        scratch_shapes=[pltpu.VMEM((D, 3 * D), f32)],
        compiler_params=params("arbitrary"),
        cost_estimate=pl.CostEstimate(
            flops=2 * rows * D * 3 * D, bytes_accessed=rows * D * 8, transcendentals=0
        ),
    )(a1, dq, dk, dv)


def feature_angles(time_steps, width):
    half = width // 2
    frequency = jnp.exp(jnp.arange(half, dtype=f32) * (-math.log(10000.0) / half))
    return time_steps.astype(f32)[:, None] * frequency[None, :]


def time_features(time_steps, width):
    angles = feature_angles(time_steps, width)
    return jnp.concatenate([jnp.cos(angles), jnp.sin(angles)], axis=-1).astype(bf16)


def row_tables(seq_spans):
    row = jnp.arange(BIN, dtype=jnp.int32)[None, :, None]
    spans = seq_spans.reshape(MB, 1, SLOTS, 2)
    offset = row - spans[..., 0]
    member = (offset >= 0) & (offset < spans[..., 1])
    position = jnp.sum(jnp.where(member, offset, 0), axis=2).astype(f32).reshape(ROWS, 1)
    lane = jnp.arange(LANES, dtype=jnp.int32)[None, :]
    half = HEAD // 2
    frequency = jnp.exp((lane % half).astype(f32) * (-math.log(10000.0) / half))
    angle = position * frequency
    cosine = jnp.cos(angle)
    sine = jnp.sin(angle) * jnp.where(lane % HEAD < half, -1.0, 1.0)
    member = member.reshape(ROWS, SLOTS)
    slot = jnp.arange(LANES, dtype=jnp.int32)[None, :]
    mine = jnp.sum(jnp.where((slot[:, None, :] == jnp.arange(SLOTS)[None, :, None]), member[:, :, None], False), axis=1)
    query_mask = jnp.where(mine > 0, neg_big, 0.0).astype(bf16)
    key_mask = jnp.where((mine == 0) & (slot < SLOTS), 1.0, 0.0).astype(bf16)
    return cosine, sine, query_mask, key_mask


def page_plan(page_deal, pages_dev, shards, device):
    per_peer = pages_dev // shards
    ids = jnp.arange(pages_dev, dtype=jnp.int32)
    deal = lax.dynamic_slice_in_dim(page_deal, device * pages_dev, pages_dev)
    target = deal // pages_dev
    earlier = (target[:, None] == target[None, :]) & (deal[None, :] < deal[:, None])
    send_pos = target * per_peer + jnp.sum(earlier.astype(jnp.int32), axis=1)
    send_order = jnp.sum(jnp.where(send_pos[None, :] == ids[:, None], ids[None, :], 0), axis=1)
    all_ids = jnp.arange(page_deal.shape[0], dtype=jnp.int32)
    hit = page_deal[None, :] == (device * pages_dev + ids)[:, None]
    owned = jnp.sum(jnp.where(hit, all_ids[None, :], 0), axis=1)
    source = owned // pages_dev
    before = (source[:, None] == source[None, :]) & (ids[None, :] < ids[:, None])
    recv_pos = source * per_peer + jnp.sum(before.astype(jnp.int32), axis=1)
    recv_order = jnp.sum(jnp.where(recv_pos[None, :] == ids[:, None], ids[None, :], 0), axis=1)
    return send_pos, send_order, recv_pos, recv_order


def pages(values):
    return values.reshape(-1, PAGE, D)


def exchange(values, shards):
    sent = values.reshape(shards, -1, PAGE, D)
    got = lax.all_to_all(sent, AXES, split_axis=0, concat_axis=0, tiled=True)
    return got.reshape(-1, PAGE, D)


def per_device(
    x_given, cotangent, norm_gain, w_qkv, w_out, w_ada, w_up, w_down, seq_spans, time_steps, page_deal
):
    shards = lax.axis_size(AXES)
    device = lax.axis_index(AXES)
    rows_dev = x_given.shape[0]
    pages_dev = rows_dev // PAGE
    send_pos, send_order, recv_pos, recv_order = page_plan(page_deal, pages_dev, shards, device)
    own = norm_gain.shape[0]
    parts = FF // D
    x_sent, w_up, w_down = lax.optimization_barrier((pages(x_given)[send_order], w_up, w_down))
    x_got = exchange(x_sent, shards)
    dy_sent, x_got = lax.optimization_barrier((pages(cotangent)[send_order], x_got))
    dy_got = exchange(dy_sent, shards)
    x = x_got[recv_pos].reshape(rows_dev, D)

    def gather(*ws):
        return lax.all_gather(jnp.concatenate(ws, axis=1), AXES, axis=0, tiled=True)

    def reduce(g):
        return lax.optimization_barrier(lax.psum_scatter(g, AXES, scatter_dimension=0, tiled=True))

    up_own = w_up.reshape(own, shards, parts, own).transpose(0, 2, 1, 3).reshape(own, FF)
    down_own = w_down.reshape(parts, own, D).transpose(1, 0, 2).reshape(own, FF)
    first_all = gather(w_qkv, w_ada, jnp.broadcast_to(norm_gain[:, None], (own, LANES)))
    second_all = gather(up_own, down_own, w_out)
    ada_all = first_all[:, 3 * D : 6 * D]
    gain = jnp.broadcast_to(first_all[:, 6 * D].astype(f32)[None, :], (8, D))

    cosine, sine, query_mask, key_mask = row_tables(seq_spans)
    time_feat = time_features(time_steps, D)
    ada_seq = jnp.dot(time_feat, ada_all, preferred_element_type=f32)
    ada_seq = jnp.concatenate([ada_seq, jnp.zeros_like(ada_seq)], axis=0)
    feat = jnp.concatenate([time_feat, jnp.zeros_like(time_feat)], axis=0)
    feat = jnp.concatenate([feat, feat], axis=0)

    qkv, a1 = qkv_call(x, gain, first_all, cosine, sine)
    p, o, rl = attend_call(qkv, query_mask, key_mask)
    dy_got, o, ada_seq = lax.optimization_barrier((dy_got, o, ada_seq))
    dy = dy_got[recv_pos].reshape(rows_dev, D)
    y, dx1, do, grads = rows_call(seq_spans, x, o, dy, ada_seq, feat, second_all)

    y_sent, do = lax.optimization_barrier((pages(y)[recv_order], do))
    y_got = exchange(y_sent, shards)
    grads = reduce(grads)

    dq, dk, dv = attend_back_call(qkv, do, o, rl, p, cosine, sine)
    dq, y_got = lax.optimization_barrier((dq, y_got))
    dx, gg = qkv_back_call(x, dx1, dq, dk, dv, gain, first_all)
    dx_sent = pages(dx)[recv_order]
    output = y_got[send_pos].reshape(rows_dev, D)
    gq = qkv_grad_call(a1, dq, dk, dv)
    gq = jnp.concatenate([gq, jnp.broadcast_to(gg[0].astype(bf16)[:, None], (D, GAIN_COLS))], axis=1)
    gq, grads, dx_sent = lax.optimization_barrier((gq, grads, dx_sent))
    gq = reduce(gq)
    input_grad = exchange(dx_sent, shards)[send_pos].reshape(rows_dev, D)
    up_grad = grads[:, :FF].reshape(own, parts, shards, own).transpose(0, 2, 1, 3).reshape(own, FF)
    down_grad = grads[:, FF : 2 * FF].reshape(own, parts, D).transpose(1, 0, 2).reshape(parts * own, D)
    return (
        output,
        input_grad,
        gq[:, 3 * D].astype(f32),
        gq[:, : 3 * D].astype(f32),
        grads[:, 2 * FF : 2 * FF + D].astype(f32),
        grads[:, 2 * FF + D :].astype(f32),
        up_grad.astype(f32),
        down_grad.astype(f32),
    )


def solution(mesh):
    placed = P(AXES, None)
    vector = P(AXES)
    return jax.shard_map(
        per_device,
        mesh=mesh,
        in_specs=(placed, placed, vector, placed, placed, placed, placed, placed, placed, vector, P()),
        out_specs=(placed, placed, vector, placed, placed, placed, placed, placed),
        check_vma=False,
    )
```
